32 devices in a mesh: cell: 8 (over y, x, core), view: 4 (over z).
Axes of the slice: x: 2, y: 2, z: 4, core: 2. Of those that a mesh axis runs over, the one named last changes fastest.
Arguments:
- attributes: float32 [14, 65536], P(None, ('cell', 'view'))
- tile_anchor: float32 [2, 1536], P(None, ('cell', 'view')), may hold values from -2 to 4
- target: float32 [1536, 4, 256], P(('cell', 'view'))
- preconditioner: float32 [14, 14, 65536], P(None, None, ('cell', 'view')), as said below
- send_index: int32 [32, 32, 96], P(('cell', 'view')), may hold values from 0 to 2047, as said below
- tile_list: int32 [1536, 64], P(('cell', 'view')), may hold values from 0 to 3071, as said below
- pair_index: int32 [1536], P(('cell', 'view')), may hold values from 0 to 47, as said below
Outputs:
- update: float32 [14, 65536], P(None, ('cell', 'view'))
- step_residual: float32 [14, 65536], P(None, ('cell', 'view'))
The draws below stay inside these ranges and needn't reach their ends.
Inputs may be any that keep to these rules, and one draw needn't show every extreme that they name: `send_index`: for each pair of devices, the 96 local Gaussian numbers that one sends to the other are distinct. `tile_list`: entries number a device's received rows by source device, then slot (96 a source); on each device the entries of its tiles are a permutation of those row numbers. `pair_index`: on each device, a permutation of its tiles' local numbers. `preconditioner`: each 14 x 14 block is symmetric and diagonally dominant with a positive diagonal.
All inputs are finite; a program needn't handle non-finite values.
Results may differ from the reference program's by a relative error of at most 0.0003.
Values sent between devices are 32-bit elements; how exact they have to be, the bound alone decides.
No kernel may reach another device: no remote copies, remote signals or barrier semaphores. Data moves between devices by JAX's collectives and lax.ppermute only.
A program may use at most 128 MiB of HBM per device.

```python
import math
import jax
import jax.numpy as jnp
from jax import lax

TILES_DEV = 48
G_DEV = 2048
ITERS = 2
TILES = 1536
G = 65536
SLOTS = 96
N_CELL = 8
N_VIEW = 4
DEVICES = 32


def draw_attributes(key, part):
    subkeys = jax.random.split(jax.random.fold_in(key, 11), 6)
    position_xy = jax.random.uniform(subkeys[0], (2, G), minval=2.0, maxval=14.0)
    position_z = jax.random.uniform(subkeys[1], (1, G), minval=0.0, maxval=8.0)
    diagonal = jax.random.uniform(subkeys[2], (3, G), minval=0.0, maxval=1.0)
    off_diagonal = 0.6 * jnp.clip(jax.random.normal(subkeys[3], (3, G)), -3.0, 3.0)
    opacity = -2.0 + 0.6 * jnp.clip(jax.random.normal(subkeys[4], (1, G)), -3.0, 3.0)
    colours = jax.random.uniform(subkeys[5], (4, G), minval=0.0, maxval=1.0)
    stacked = jnp.concatenate([position_xy, position_z, diagonal[0:1], off_diagonal[0:1], diagonal[1:2], off_diagonal[1:3], diagonal[2:3], opacity, colours], axis=0)
    return stacked.astype(jnp.float32)


def draw_target(key, part):
    growth = 1.0 + 2.0 * jnp.arange(TILES, dtype=jnp.float32) / TILES
    noise = 0.4 + 0.25 * jax.random.normal(jax.random.fold_in(key, 12), (TILES, 4, 256))
    return (noise * growth[:, None, None]).astype(jnp.float32)


def draw_preconditioner(key, part):
    subkeys = jax.random.split(jax.random.fold_in(key, 13), 2)
    noise = 0.08 * jax.random.normal(subkeys[0], (14, 14, G))
    identity = jnp.eye(14, dtype=jnp.float32)
    symmetric = 0.5 * (noise + noise.transpose(1, 0, 2)) * (1.0 - identity)[:, :, None]
    row_total = jnp.sum(jnp.abs(symmetric), axis=1)
    diagonal = row_total + jax.random.uniform(subkeys[1], (14, G), minval=0.5, maxval=2.0)
    return (symmetric + identity[:, :, None] * diagonal[:, None, :]).astype(jnp.float32)


def draw_send_index(key, part):
    upper = 2 ** 30 // G_DEV
    scores = jax.random.randint(jax.random.fold_in(key, 14), (DEVICES, DEVICES, G_DEV), 0, upper) * G_DEV + jnp.arange(G_DEV, dtype=jnp.int32)
    scores = scores.at[0, 0, G_DEV - 1].set(2 ** 30 + 1)
    scores = scores.at[0, DEVICES - 1, 0].set(2 ** 30)
    _, picked = lax.top_k(scores, SLOTS)
    return picked.astype(jnp.int32)


def draw_tile_list(key, part):
    subkeys = jax.random.split(jax.random.fold_in(key, 15), DEVICES)
    listed = jax.vmap(lambda single: jax.random.permutation(single, TILES_DEV * 64))(subkeys)
    return listed.reshape(TILES, 64).astype(jnp.int32)


def draw_pair_index(key, part):
    subkeys = jax.random.split(jax.random.fold_in(key, 16), DEVICES)
    paired = jax.vmap(lambda single: jax.random.permutation(single, TILES_DEV))(subkeys)
    return paired.reshape(TILES).astype(jnp.int32)


def block_scale(own_key, dims, pieces, smallest, high):
    def one(position, shards_of):
        heights = jax.random.uniform(jax.random.fold_in(jax.random.fold_in(own_key, 6), position), (shards_of,), jnp.float32, smallest / len(pieces), high / len(pieces))
        return jnp.repeat(jnp.exp(heights), dims[position] // shards_of).reshape((-1,) + (1,) * (len(dims) - position - 1))

    level = one(*pieces[0])
    for cut in pieces[1:]:
        level = level * one(*cut)
    return level


def setup_inputs(seed: int = 0) -> dict:
    keys = jax.random.split(jax.random.key(seed), 8)
    return {
        "attributes": draw_attributes(jax.random.fold_in(keys[7], 71), 0),
        "tile_anchor": jnp.clip(-2.0 + 6.0 * jax.random.uniform(keys[1], (2, TILES), jnp.float32) ** block_scale(keys[1], (2, TILES), ((1, 32),), -0.2, 0.2), -2.0, 4.0),
        "target": draw_target(jax.random.fold_in(keys[7], 71), 0),
        "preconditioner": draw_preconditioner(jax.random.fold_in(keys[7], 71), 0),
        "send_index": draw_send_index(jax.random.fold_in(keys[7], 71), 0),
        "tile_list": draw_tile_list(jax.random.fold_in(keys[7], 71), 0),
        "pair_index": draw_pair_index(jax.random.fold_in(keys[7], 71), 0),
    }


DAMPING = 0.5
PRIOR_WEIGHT = 0.3
DILATION = 0.3

def camera_axes():
    tilt_cos, tilt_sin = (math.cos(0.3), math.sin(0.3))
    turn_cos, turn_sin = (math.cos(0.2), math.sin(0.2))
    return ((turn_cos, turn_sin * tilt_sin, turn_sin * tilt_cos), (0.0, tilt_cos, -tilt_sin), (-turn_sin, turn_cos * tilt_sin, turn_cos * tilt_cos))

def render(listed, anchor):
    camera = camera_axes()
    factor_rows = ((jnp.exp(listed[3]), None, None), (listed[4], jnp.exp(listed[5]), None), (listed[6], listed[7], jnp.exp(listed[8])))
    screen = []
    for axis_row in range(2):
        place_value = camera[axis_row][0] * listed[0] + camera[axis_row][1] * listed[1] + camera[axis_row][2] * listed[2]
        screen.append(place_value - anchor[axis_row][:, None])
    depth_values = camera[2][0] * listed[0] + camera[2][1] * listed[1] + camera[2][2] * listed[2]
    projected = []
    for axis_row in range(2):
        row_terms = []
        for column_index in range(3):
            total_term = camera[axis_row][column_index] * factor_rows[column_index][column_index]
            for inner_index in range(column_index + 1, 3):
                total_term = total_term + camera[axis_row][inner_index] * factor_rows[inner_index][column_index]
            row_terms.append(total_term)
        projected.append(row_terms)
    cov_xx = projected[0][0] * projected[0][0] + projected[0][1] * projected[0][1] + projected[0][2] * projected[0][2] + DILATION
    cov_xy = projected[0][0] * projected[1][0] + projected[0][1] * projected[1][1] + projected[0][2] * projected[1][2]
    cov_yy = projected[1][0] * projected[1][0] + projected[1][1] * projected[1][1] + projected[1][2] * projected[1][2] + DILATION
    determinant = cov_xx * cov_yy - cov_xy * cov_xy
    conic_xx = (cov_yy / determinant)[..., None]
    conic_xy = (-cov_xy / determinant)[..., None]
    conic_yy = (cov_xx / determinant)[..., None]
    opacity = 0.99 * jax.nn.sigmoid(listed[9])
    pixels = jnp.arange(256)
    pixel_x = (pixels % 16).astype(jnp.float32) + 0.5
    pixel_y = (pixels // 16).astype(jnp.float32) + 0.5
    offset_x = pixel_x - screen[0][:, :, None]
    offset_y = pixel_y - screen[1][:, :, None]
    exponent = -0.5 * (conic_xx * offset_x * offset_x + 2.0 * conic_xy * offset_x * offset_y + conic_yy * offset_y * offset_y)
    coverage = opacity[..., None] * jnp.exp(exponent)
    log_keep = jnp.log1p(-coverage)
    earlier = (jnp.arange(64)[None, :] < jnp.arange(64)[:, None]).astype(jnp.float32)
    before = jnp.einsum('jk,bkp->bjp', earlier, log_keep, precision=lax.Precision.HIGHEST)
    weight = jnp.exp(before) * coverage
    colours = jnp.einsum('cbk,bkp->bcp', listed[10:14], weight, precision=lax.Precision.HIGHEST)
    depths = jnp.einsum('bk,bkp->bp', depth_values, weight, precision=lax.Precision.HIGHEST)
    return (colours, depths)

def reference(attributes, tile_anchor, target, preconditioner, send_index, tile_list, pair_index):
    devices = N_CELL * N_VIEW
    tile_device = jnp.arange(TILES, dtype=jnp.int32) // TILES_DEV
    source = tile_list // SLOTS
    slot_number = tile_list % SLOTS
    gaussian = source * G_DEV + send_index[source, tile_device[:, None], slot_number]
    view_index = tile_device % N_VIEW
    partner_device = tile_device - view_index + (view_index + 1) % N_VIEW
    partner = partner_device * TILES_DEV + pair_index
    blocks = gaussian.reshape(devices, TILES_DEV, 64)
    anchors = tile_anchor.reshape(2, devices, TILES_DEV).transpose(1, 0, 2)

    def forward(block_args):
        listed_ids, anchor = block_args
        return render(attributes[:, listed_ids], anchor)
    colours, depths = lax.map(forward, (blocks, anchors))
    colours = colours.reshape(TILES, 4, 256)
    depths = depths.reshape(TILES, 256)

    def tangent_image(tangent):

        def one_block(block_args):
            listed_ids, anchor = block_args
            return jax.jvp(lambda values: render(values, anchor), (attributes[:, listed_ids],), (tangent[:, listed_ids],))[1]
        colour_tangent, depth_tangent = lax.map(one_block, (blocks, anchors))
        return (colour_tangent.reshape(TILES, 4, 256), depth_tangent.reshape(TILES, 256))

    def pull_back(colour_cot, depth_cot):
        colour_blocks = colour_cot.reshape(devices, TILES_DEV, 4, 256)
        depth_blocks = depth_cot.reshape(devices, TILES_DEV, 256)

        def one_block(block_args):
            listed_ids, anchor, colour_part, depth_part = block_args
            _, pullback = jax.vjp(lambda values: render(values, anchor), attributes[:, listed_ids])
            return pullback((colour_part, depth_part))[0]
        cotangent = lax.map(one_block, (blocks, anchors, colour_blocks, depth_blocks))
        flattened = cotangent.transpose(0, 2, 3, 1).reshape(-1, 14)
        return jax.ops.segment_sum(flattened, gaussian.reshape(-1), num_segments=G).T

    def depth_cotangent(prior_term):
        shifted = jnp.zeros_like(prior_term).at[partner].add(prior_term)
        return PRIOR_WEIGHT * prior_term - PRIOR_WEIGHT * shifted

    def normal_product(vector):
        colour_tangent, depth_tangent = tangent_image(vector)
        prior_tangent = PRIOR_WEIGHT * (depth_tangent - depth_tangent[partner])
        return pull_back(colour_tangent, depth_cotangent(prior_tangent)) + DAMPING * vector

    def apply_scaling(vector):
        return jnp.einsum('ijg,jg->ig', preconditioner, vector, precision=lax.Precision.HIGHEST)
    photometric = colours - target
    prior_term = PRIOR_WEIGHT * (depths - depths[partner])
    gradient = pull_back(photometric, depth_cotangent(prior_term))
    residual = -gradient
    solution = jnp.zeros_like(attributes)
    scaled = apply_scaling(residual)
    direction = scaled
    scaled_norm = jnp.sum(residual * scaled)
    for iteration in range(ITERS):
        normal_image = normal_product(direction)
        step_size = scaled_norm / jnp.sum(direction * normal_image)
        solution = solution + step_size * direction
        residual = residual - step_size * normal_image
        if iteration + 1 < ITERS:
            scaled = apply_scaling(residual)
            next_norm = jnp.sum(residual * scaled)
            direction = scaled + next_norm / scaled_norm * direction
            scaled_norm = next_norm
    return (solution, residual)
```

```python
import functools
import math

import jax
import jax.numpy as jnp
from jax import lax
from jax.experimental import pallas as pl
from jax.experimental.pallas import tpu as pltpu
from jax.sharding import PartitionSpec as P

ITERS = 2
DAMPING = 0.5
PRIOR_WEIGHT = 0.3
DILATION = 0.3

F32 = jnp.float32
BF16 = jnp.bfloat16
LANES = 128
ROWS = 16
SCALAR = 6
ACTIVE = (0, 1, 2, 3, 4, 5, 6, 8, 9, 10, 11, 12)
KSLOTS = 64
PIXELS = 256
ATTRS = 14


def camera_axes():
    tilt_cos, tilt_sin = (math.cos(0.3), math.sin(0.3))
    turn_cos, turn_sin = (math.cos(0.2), math.sin(0.2))
    return (
        (turn_cos, turn_sin * tilt_sin, turn_sin * tilt_cos),
        (0.0, tilt_cos, -tilt_sin),
        (-turn_sin, turn_cos * tilt_sin, turn_cos * tilt_cos),
    )


CAM = camera_axes()


def payload_rows(slots):
    return -(-len(ACTIVE) * slots // LANES)


def iota(shape, dim):
    return lax.broadcasted_iota(jnp.int32, shape, dim)


def split(value, parts):
    pieces = []
    for _ in range(parts - 1):
        piece = value.astype(BF16)
        pieces.append(piece)
        value = value - piece.astype(F32)
    pieces.append(value.astype(BF16))
    return pieces


def dot(a, b):
    return jnp.dot(a, b, preferred_element_type=F32)


def dot_nt(a, b):
    return lax.dot_general(a, b, (((1,), (1,)), ((), ())), preferred_element_type=F32)


def total(value):
    return jnp.sum(jnp.sum(value, axis=0, keepdims=True), axis=1, keepdims=True)


def pack(feature, out_ref, count, slots):
    depth = payload_rows(slots)
    lane = iota((count, LANES), 1)
    rows = [jnp.zeros((count, LANES), F32) for _ in range(depth)]
    for place, row in enumerate(ACTIVE):
        value = feature(row)
        at, offset = divmod(place * slots, LANES)
        end = offset + slots
        if offset:
            value = pltpu.roll(value, offset, 1)
        rows[at] = jnp.where((lane >= offset) & (lane < end), value, rows[at])
        if end > LANES:
            rows[at + 1] = jnp.where(lane < end - LANES, value, rows[at + 1])
    for at in range(depth):
        out_ref[pl.ds(at, count, stride=depth), :] = rows[at]


def unpack(in_ref, count, slots):
    depth = payload_rows(slots)
    lane = iota((count, LANES), 1)
    rows = [in_ref[pl.ds(at, count, stride=depth), :] for at in range(depth)]
    features = {}
    for place, row in enumerate(ACTIVE):
        at, offset = divmod(place * slots, LANES)
        value = rows[at]
        if offset + slots > LANES:
            value = jnp.where(lane >= offset, value, rows[at + 1])
        if offset:
            value = pltpu.roll(value, LANES - offset, 1)
        features[row] = jnp.where(lane < slots, value, 0.0)
    return features


def put_features(features, ref, count):
    ref[...] = jnp.zeros(ref.shape, F32)
    for row, value in features.items():
        ref[pl.ds(row, count, stride=ROWS), :] = value


def gather(source_ref, chunks, index_a, index_b, blocks, parts, lhs_ref, out_ref):
    for part, piece in enumerate(split(source_ref[...], parts)):
        lhs_ref[:, part * LANES : (part + 1) * LANES] = piece

    def body(step, carry):
        first = 2 * step
        which_a = jnp.concatenate([index_a[pl.ds(first + i, 1), :] for i in range(2)], axis=1)
        which_b = jnp.concatenate([index_b[pl.ds(first + i, 1), :] for i in range(2)], axis=1)
        onehot = jnp.where(iota((LANES, 2 * LANES), 0) == which_b, 1.0, 0.0).astype(BF16)
        product = dot(lhs_ref[...], jnp.concatenate([onehot] * parts, axis=0))
        picked = jnp.zeros((ROWS, 2 * LANES), F32)
        for a in range(chunks):
            picked = jnp.where(which_a == a, product[a * ROWS : (a + 1) * ROWS], picked)
        start = pl.multiple_of(first * ROWS, 2 * ROWS)
        out_ref[pl.ds(start, ROWS), :] = picked[:, :LANES]
        out_ref[pl.ds(start + ROWS, ROWS), :] = picked[:, LANES:]
        return carry

    lax.fori_loop(0, blocks // 2, body, 0)


def scatter(source_ref, chunks, index_a, index_b, blocks, acc_ref):
    acc_ref[...] = jnp.zeros(acc_ref.shape, F32)
    together = 4

    def body(step, carry):
        left, right = [], []
        for i in range(together):
            at = step * together + i
            value = source_ref[pl.ds(pl.multiple_of(at * ROWS, ROWS), ROWS), :]
            pieces = split(value, 2)
            which = jnp.broadcast_to(index_a[pl.ds(at, 1), :], (ROWS, LANES)).astype(F32).astype(BF16)
            onehot = jnp.where(iota((LANES, LANES), 0) == index_b[pl.ds(at, 1), :], 1.0, 0.0).astype(BF16)
            columns = []
            for piece in pieces:
                columns.append(
                    jnp.concatenate(
                        [
                            jnp.where(which == jnp.asarray(a, BF16), piece, jnp.zeros_like(piece))
                            for a in range(chunks)
                        ],
                        axis=0,
                    )
                )
                right.append(onehot)
            left += columns
        acc_ref[...] += dot_nt(jnp.concatenate(left, axis=1), jnp.concatenate(right, axis=1))
        return carry

    lax.fori_loop(0, blocks // together, body, 0)


def geometry(attr):
    e3, e5, e8 = jnp.exp(attr(3)), jnp.exp(attr(5)), jnp.exp(attr(8))
    a4, a6, a7, a9 = attr(4), attr(6), attr(7), attr(9)
    m = [
        (
            CAM[r][0] * e3 + CAM[r][1] * a4 + CAM[r][2] * a6,
            CAM[r][1] * e5 + CAM[r][2] * a7,
            CAM[r][2] * e8,
        )
        for r in range(2)
    ]
    sxx = m[0][0] * m[0][0] + m[0][1] * m[0][1] + m[0][2] * m[0][2] + DILATION
    sxy = m[0][0] * m[1][0] + m[0][1] * m[1][1] + m[0][2] * m[1][2]
    syy = m[1][0] * m[1][0] + m[1][1] * m[1][1] + m[1][2] * m[1][2] + DILATION
    inverse = 1.0 / (sxx * syy - sxy * sxy)
    return {
        "e": (e3, e5, e8),
        "m": m,
        "q": (syy * inverse, -sxy * inverse, sxx * inverse),
        "fade": 1.0 / (1.0 + jnp.exp(a9)),
        "a9": a9,
    }


def place(value):
    return [CAM[r][0] * value(0) + CAM[r][1] * value(1) + CAM[r][2] * value(2) for r in range(3)]


def project(attr, geo):
    x, y, z = place(attr)
    a9 = geo["a9"]
    shade = math.log(0.99) - (jnp.maximum(-a9, 0.0) + jnp.log(1.0 + jnp.exp(-jnp.abs(a9))))
    rows = {0: x, 1: y, 12: z, 2: geo["q"][0], 3: geo["q"][1], 4: geo["q"][2], 5: shade}
    for band in range(4):
        rows[8 + band] = attr(10 + band)
    return rows


def project_tangent(v, geo):
    x, y, z = place(v)
    (e3, e5, e8), m, (qxx, qxy, qyy) = geo["e"], geo["m"], geo["q"]
    v3, v5, v8 = e3 * v(3), e5 * v(5), e8 * v(8)
    d = [
        (
            CAM[r][0] * v3 + CAM[r][1] * v(4) + CAM[r][2] * v(6),
            CAM[r][1] * v5 + CAM[r][2] * v(7),
            CAM[r][2] * v8,
        )
        for r in range(2)
    ]
    sxx = 2.0 * (m[0][0] * d[0][0] + m[0][1] * d[0][1] + m[0][2] * d[0][2])
    syy = 2.0 * (m[1][0] * d[1][0] + m[1][1] * d[1][1] + m[1][2] * d[1][2])
    sxy = sum(m[0][c] * d[1][c] + d[0][c] * m[1][c] for c in range(3))
    rows = {
        0: x,
        1: y,
        12: z,
        2: -(qxx * qxx * sxx + 2.0 * qxx * qxy * sxy + qxy * qxy * syy),
        3: -(qxx * qxy * sxx + (qxx * qyy + qxy * qxy) * sxy + qxy * qyy * syy),
        4: -(qxy * qxy * sxx + 2.0 * qxy * qyy * sxy + qyy * qyy * syy),
        5: geo["fade"] * v(9),
    }
    for band in range(4):
        rows[8 + band] = v(10 + band)
    return rows


def project_cotangent(t, geo):
    (e3, e5, e8), m, (qxx, qxy, qyy) = geo["e"], geo["m"], geo["q"]
    bxx, bxy, byy = t(2), t(3), t(4)
    sxx = -(qxx * qxx * bxx + qxx * qxy * bxy + qxy * qxy * byy)
    sxy = -(2.0 * qxx * qxy * bxx + (qxx * qyy + qxy * qxy) * bxy + 2.0 * qxy * qyy * byy)
    syy = -(qxy * qxy * bxx + qxy * qyy * bxy + qyy * qyy * byy)
    n0 = [2.0 * sxx * m[0][c] + sxy * m[1][c] for c in range(3)]
    n1 = [2.0 * syy * m[1][c] + sxy * m[0][c] for c in range(3)]
    x, y, z = t(0), t(1), t(12)
    out = {j: CAM[0][j] * x + CAM[1][j] * y + CAM[2][j] * z for j in range(3)}
    out[3] = e3 * (CAM[0][0] * n0[0] + CAM[1][0] * n1[0])
    out[4] = CAM[0][1] * n0[0] + CAM[1][1] * n1[0]
    out[5] = e5 * (CAM[0][1] * n0[1] + CAM[1][1] * n1[1])
    out[6] = CAM[0][2] * n0[0] + CAM[1][2] * n1[0]
    out[7] = CAM[0][2] * n0[1] + CAM[1][2] * n1[1]
    out[8] = e8 * (CAM[0][2] * n0[2] + CAM[1][2] * n1[2])
    out[9] = geo["fade"] * t(5)
    for band in range(4):
        out[10 + band] = t(8 + band)
    return out


def to_chunks(ref, chunk_ref, chunks):
    for a in range(chunks):
        chunk_ref[a * ROWS : a * ROWS + ATTRS, :] = ref[:, a * LANES : (a + 1) * LANES]


def reader(ref, count):
    return lambda row: ref[pl.ds(row, count, stride=ROWS), :]


def chunk(ref, a):
    return ref[a * ROWS : a * ROWS + ATTRS, :]


def send_rows(rows, scalar, meta, sa_ref, sb_ref, source_ref, lhs_ref, sent_ref, out_ref, parts):
    chunks, devices, slots = meta
    put_features(rows, source_ref, chunks)
    gather(source_ref, chunks, sa_ref, sb_ref, devices, parts, lhs_ref, sent_ref)

    def feature(row):
        if row == SCALAR:
            return jnp.broadcast_to(scalar, (devices, LANES))
        return sent_ref[pl.ds(row, devices, stride=ROWS), :]

    pack(feature, out_ref, devices, slots)


def first_owner(meta, attr_ref, sa_ref, sb_ref, out_ref, chunk_ref, source_ref, lhs_ref, sent_ref):
    chunks = meta[0]
    to_chunks(attr_ref, chunk_ref, chunks)
    attr = reader(chunk_ref, chunks)
    rows = project(attr, geometry(attr))
    send_rows(rows, jnp.zeros((1, 1), F32), meta, sa_ref, sb_ref, source_ref, lhs_ref, sent_ref, out_ref, 3)


def receive_cotangent(meta, recv_ref, sa_ref, sb_ref, sent_ref, acc_ref, grad_ref, geo):
    chunks, devices, slots = meta
    features = unpack(recv_ref, devices, slots)
    put_features(features, sent_ref, devices)
    scatter(sent_ref, chunks, sa_ref, sb_ref, devices, acc_ref)
    for j, value in project_cotangent(reader(acc_ref, chunks), geo).items():
        grad_ref[pl.ds(j, chunks, stride=ROWS), :] = value
    return features[SCALAR]


def first_lane(value):
    return total(jnp.where(iota(value.shape, 1) == 0, value, 0.0))


def apply_scaling(pre_ref, source_ref, a):
    result = None
    for i in range(ATTRS):
        term = pre_ref[i, :, a * LANES : (a + 1) * LANES] * source_ref[a * ROWS + i : a * ROWS + i + 1, :]
        result = term if result is None else result + term
    return result


def owner_step(
    meta, first, recv_ref, attr_ref, pre_ref, sa_ref, sb_ref, *rest
):
    if first:
        (out_ref, res_out, dir_out, chunk_ref, source_ref, lhs_ref, sent_ref, acc_ref, grad_ref, dir_ref) = rest
    else:
        (
            res_in, dir_in, sc_ref,
            out_ref, res_out, sol_out, dir_out,
            chunk_ref, source_ref, lhs_ref, sent_ref, acc_ref, grad_ref, dir_ref,
        ) = rest
    chunks, devices, slots = meta
    to_chunks(attr_ref, chunk_ref, chunks)
    attr = reader(chunk_ref, chunks)
    geo = geometry(attr)
    scalars = receive_cotangent(meta, recv_ref, sa_ref, sb_ref, sent_ref, acc_ref, grad_ref, geo)
    if not first:
        step = sc_ref[0:1, 0:1] / first_lane(scalars)
    norm = jnp.zeros((ATTRS, LANES), F32)
    for a in range(chunks):
        here = slice(a * LANES, (a + 1) * LANES)
        if first:
            residual = -chunk(grad_ref, a)
        else:
            before = dir_in[:, here]
            image = chunk(grad_ref, a) + DAMPING * before
            residual = res_in[:, here] - step * image
            sol_out[:, here] = step * before
        res_out[:, here] = residual
        grad_ref[a * ROWS : a * ROWS + ATTRS, :] = residual
        scaled = apply_scaling(pre_ref, grad_ref, a)
        dir_out[:, here] = scaled
        dir_ref[a * ROWS : a * ROWS + ATTRS, :] = scaled
        norm = norm + residual * scaled
    rows = project_tangent(reader(dir_ref, chunks), geo)
    send_rows(rows, total(norm), meta, sa_ref, sb_ref, source_ref, lhs_ref, sent_ref, out_ref, 2)


def last_owner(
    meta, recv_ref, attr_ref, sa_ref, sb_ref, res_in, sol_in, dir_in, sc_ref,
    sol_out, res_out, chunk_ref, sent_ref, acc_ref, grad_ref,
):
    chunks, devices, slots = meta
    to_chunks(attr_ref, chunk_ref, chunks)
    geo = geometry(reader(chunk_ref, chunks))
    scalars = receive_cotangent(meta, recv_ref, sa_ref, sb_ref, sent_ref, acc_ref, grad_ref, geo)
    step = sc_ref[0:1, 0:1] / first_lane(scalars)
    for a in range(chunks):
        here = slice(a * LANES, (a + 1) * LANES)
        direction = dir_in[:, here]
        image = chunk(grad_ref, a) + DAMPING * direction
        sol_out[:, here] = sol_in[:, here] + step * direction
        res_out[:, here] = res_in[:, here] - step * image


def pixel_basis(shape, pixel_dim, term_dim):
    pixel, term = iota(shape, pixel_dim), iota(shape, term_dim) & 7
    x = (pixel & 15).astype(F32) - 7.5
    y = (pixel >> 4).astype(F32) - 7.5
    value = jnp.zeros(shape, F32)
    for m, field in enumerate((jnp.ones(shape, F32), x, y, x * x, x * y, y * y)):
        value = jnp.where(term == m, field, value)
    return value


def triangle(rows, later):
    shape = (rows, LANES)
    row, column = iota(shape, 0) & (LANES - 1), iota(shape, 1)
    same = (row >> 6) == (column >> 6)
    order = (row > column) if later else (row < column)
    return jnp.where(same & order, 1.0, 0.0).astype(BF16)


def put_terms(terms, ref, blocks):
    ref[...] = jnp.zeros(ref.shape, F32)
    for m, term in enumerate(terms):
        for part, piece in enumerate(split(term, 3)):
            ref[pl.ds(part * 8 + m, blocks, stride=32), :] = piece.astype(F32)


def forward_basis():
    return jnp.where(iota((PIXELS, 32), 1) < 24, pixel_basis((PIXELS, 32), 0, 1), 0.0).astype(BF16)


def two_tiles(value):
    low = iota((8, LANES), 1) < KSLOTS
    return jnp.concatenate([jnp.where(low, value, 0.0), jnp.where(low, 0.0, value)], axis=0)


def stacked_lhs(value):
    high, low = split(value, 2)
    return jnp.concatenate(
        [jnp.concatenate([high, high], axis=1), jnp.concatenate([low, jnp.zeros_like(low)], axis=1)], axis=0
    )


def fold(value):
    half = value.shape[0] // 2
    return value[:half] + value[half:]


def local_place(theta, ax_ref, ay_ref):
    return theta(0) - ax_ref[...] - 8.0, theta(1) - ay_ref[...] - 8.0


def send_order(pr_ref, depth, ds_ref):
    tiles = depth.shape[0]
    onehot = jnp.where(iota((tiles, tiles), 0) == pr_ref[...], 1.0, 0.0).astype(BF16)
    ds_ref[...] = sum(dot(onehot, piece) for piece in split(depth, 3))


def receive_rows(meta, recv_ref, ta_ref, tb_ref, source_ref, lhs_ref, out_ref, parts):
    blocks, devices, slots = meta
    features = unpack(recv_ref, devices, slots)
    put_features(features, source_ref, devices)
    gather(source_ref, devices, ta_ref, tb_ref, blocks, parts, lhs_ref, out_ref)
    return features[SCALAR]


def tile_forward(
    meta, recv_ref, ta_ref, tb_ref, ax_ref, ay_ref, target_ref, pr_ref,
    theta_ref, w_ref, rho_ref, j_ref, d_ref, ds_ref,
    source_ref, lhs_ref, term_ref,
):
    blocks, devices, slots = meta
    receive_rows(meta, recv_ref, ta_ref, tb_ref, source_ref, lhs_ref, theta_ref, 3)
    theta = reader(theta_ref, blocks)
    dx, dy = local_place(theta, ax_ref, ay_ref)
    qxx, qxy, qyy = theta(2), theta(3), theta(4)
    gx, gy = qxx * dx + qxy * dy, qxy * dx + qyy * dy
    terms = (theta(5) - 0.5 * (dx * gx + dy * gy), gx, gy, -0.5 * qxx, -qxy, -0.5 * qyy)
    put_terms(terms, term_ref, blocks)
    basis = forward_basis()
    earlier = triangle(3 * LANES, False)

    def body(block, carry):
        coefficients = term_ref[pl.ds(pl.multiple_of(block * 32, 32), 32), :].astype(BF16)
        exponent = dot(basis, coefficients)
        coverage = jnp.exp(exponent)
        log_keep = jnp.log(1.0 - coverage)
        before = dot(jnp.concatenate(split(log_keep, 3), axis=1), earlier)
        weight = jnp.exp(before) * coverage
        w_ref[block] = weight
        rho_ref[block] = jnp.exp(exponent - log_keep)
        start = pl.multiple_of(block * ROWS, ROWS)
        left = stacked_lhs(two_tiles(theta_ref[pl.ds(start + 8, 8), :]))
        image = fold(dot_nt(left, jnp.concatenate(split(weight, 2), axis=1)))
        j_ref[pl.ds(start, ROWS), :] = image
        j_ref[pl.ds(start, 4), :] = image[0:4] - target_ref[2 * block]
        j_ref[pl.ds(start + 8, 4), :] = image[8:12] - target_ref[2 * block + 1]
        d_ref[pl.ds(2 * block, 1), :] = image[4:5]
        d_ref[pl.ds(2 * block + 1, 1), :] = image[12:13]
        return carry

    lax.fori_loop(0, blocks, body, 0)
    send_order(pr_ref, d_ref[...], ds_ref)


def tile_tangent(meta, first, recv_ref, ta_ref, tb_ref, ax_ref, ay_ref, pr_ref, theta_ref, w_ref, rho_ref, *rest):
    if first:
        j_ref, d_ref, ds_ref, sc_ref, source_ref, lhs_ref, term_ref, dot_ref = rest
    else:
        j_in, d_in, sc_in, j_ref, d_ref, ds_ref, sc_ref, source_ref, lhs_ref, term_ref, dot_ref = rest
    blocks, devices, slots = meta
    norm = first_lane(receive_rows(meta, recv_ref, ta_ref, tb_ref, source_ref, lhs_ref, dot_ref, 2))
    if not first:
        ratio = norm / sc_in[0:1, 0:1]
        sc_ref[8:16, :] = jnp.broadcast_to(ratio, (8, LANES))
    else:
        sc_ref[8:16, :] = jnp.zeros((8, LANES), F32)
    sc_ref[0:8, :] = jnp.broadcast_to(norm, (8, LANES))
    theta, tangent = reader(theta_ref, blocks), reader(dot_ref, blocks)
    dx, dy = local_place(theta, ax_ref, ay_ref)
    qxx, qxy, qyy = theta(2), theta(3), theta(4)
    gx, gy = qxx * dx + qxy * dy, qxy * dx + qyy * dy
    tx, ty, txx, txy, tyy = (tangent(row) for row in range(5))
    hx = txx * dx + txy * dy + qxx * tx + qxy * ty
    hy = txy * dx + tyy * dy + qxy * tx + qyy * ty
    constant = tangent(5) - 0.5 * (tx * gx + dx * hx + ty * gy + dy * hy)
    put_terms((constant, hx, hy, -0.5 * txx, -txy, -0.5 * tyy), term_ref, blocks)
    basis = forward_basis()
    earlier = triangle(2 * LANES, False)

    def body(block, carry):
        coefficients = term_ref[pl.ds(pl.multiple_of(block * 32, 32), 32), :].astype(BF16)
        change = dot(basis, coefficients)
        weight = w_ref[block]
        before = dot(jnp.concatenate(split(rho_ref[block] * change, 2), axis=1), earlier)
        weight_change = weight * (change - before)
        start = pl.multiple_of(block * ROWS, ROWS)
        left = stacked_lhs(two_tiles(theta_ref[pl.ds(start + 8, 8), :]))
        left_change = stacked_lhs(two_tiles(dot_ref[pl.ds(start + 8, 8), :]))
        image = fold(
            dot_nt(left, jnp.concatenate(split(weight_change, 2), axis=1))
            + dot_nt(left_change, jnp.concatenate(split(weight, 2), axis=1))
        )
        if not first:
            image = image + ratio * j_in[pl.ds(start, ROWS), :]
        j_ref[pl.ds(start, ROWS), :] = image
        d_ref[pl.ds(2 * block, 1), :] = image[4:5]
        d_ref[pl.ds(2 * block + 1, 1), :] = image[12:13]
        return carry

    lax.fori_loop(0, blocks, body, 0)
    send_order(pr_ref, d_ref[...], ds_ref)


def tile_pull(
    meta, mode, j_ref, d_ref, next_ref, past_ref, pc_ref, ta_ref, tb_ref, ax_ref, ay_ref, theta_ref, w_ref, rho_ref, *rest
):
    if mode == 0:
        out_ref, depth_ref, term_ref, bar_ref, acc_ref = rest
    elif mode == 1:
        dir_in, out_ref, depth_ref, term_ref, bar_ref, acc_ref = rest
    else:
        scaled_in, dir_in, sc_ref, out_ref, dir_out, depth_ref, term_ref, bar_ref, acc_ref = rest
    blocks, devices, slots = meta
    tiles = 2 * blocks
    depth = d_ref[...]
    onehot = jnp.where(iota((tiles, tiles), 1) == pc_ref[...], 1.0, 0.0).astype(BF16)
    partner = sum(dot(onehot, piece) for piece in split(next_ref[...], 3))
    prior = PRIOR_WEIGHT * (depth - partner)
    prior_past = PRIOR_WEIGHT * (past_ref[...] - depth)
    depth_ref[...] = PRIOR_WEIGHT * prior - PRIOR_WEIGHT * prior_past
    later = triangle(2 * LANES, True)
    moments = pixel_basis((ROWS, PIXELS), 1, 0)
    moments = jnp.where(iota((ROWS, PIXELS), 0) < 8, moments, 0.0).astype(BF16)
    moments = jnp.concatenate([moments, moments], axis=1)
    row = iota((ROWS, PIXELS), 0)
    low = iota((8, LANES), 1) < KSLOTS

    def body(block, energy):
        start = pl.multiple_of(block * ROWS, ROWS)
        image = j_ref[pl.ds(start, ROWS), :]
        energy = energy + jnp.where((row & 7) < 4, image * image, 0.0)
        cotangent = jnp.where(row == 4, depth_ref[pl.ds(2 * block, 1), :], image)
        cotangent = jnp.where(row == 12, depth_ref[pl.ds(2 * block + 1, 1), :], cotangent)
        weight = w_ref[block]
        colours = two_tiles(theta_ref[pl.ds(start + 8, 8), :])
        cot_high, cot_low = split(cotangent, 2)
        col_high, col_low = split(colours, 2)
        across = jnp.concatenate([cot_high.astype(F32), cot_low.astype(F32), cot_high.astype(F32)], axis=0).T
        pulled = dot(across.astype(BF16), jnp.concatenate([col_high, col_high, col_low], axis=0))
        share = weight * pulled
        after = dot(jnp.concatenate(split(share, 2), axis=1), later)
        bar = share - rho_ref[block] * after
        bar_moments = dot(moments, jnp.concatenate(split(bar, 2), axis=0))
        left = jnp.concatenate(
            [
                jnp.concatenate([cot_high, cot_high], axis=1),
                jnp.concatenate([cot_low, jnp.zeros_like(cot_low)], axis=1),
            ],
            axis=0,
        )
        colour_bar = fold(dot(left, jnp.concatenate(split(weight, 2), axis=0)))
        term_ref[pl.ds(start, 8), :] = bar_moments[0:8]
        bar_ref[pl.ds(start + 8, 8), :] = jnp.where(low, colour_bar[0:8], colour_bar[8:16])
        return energy

    energy = lax.fori_loop(0, blocks, body, jnp.zeros((ROWS, PIXELS), F32))
    scalar = jnp.zeros((1, 1), F32)
    if mode:
        if mode == 1:
            direction = dir_in[...]
        else:
            direction = scaled_in[...] + sc_ref[8:9, 0:1] * dir_in[...]
            dir_out[...] = direction
        scalar = total(energy) + total(prior * prior) + DAMPING * total(direction * direction)
    theta, bars = reader(theta_ref, blocks), reader(term_ref, blocks)
    dx, dy = local_place(theta, ax_ref, ay_ref)
    qxx, qxy, qyy = theta(2), theta(3), theta(4)
    gx, gy = qxx * dx + qxy * dy, qxy * dx + qyy * dy
    b0 = bars(0)
    hx, hy = bars(1) - 0.5 * dx * b0, bars(2) - 0.5 * dy * b0
    values = (
        -0.5 * gx * b0 + qxx * hx + qxy * hy,
        -0.5 * gy * b0 + qxy * hx + qyy * hy,
        dx * hx - 0.5 * bars(3),
        dy * hx + dx * hy - bars(4),
        dy * hy - 0.5 * bars(5),
        b0,
        jnp.zeros_like(b0),
        jnp.zeros_like(b0),
    )
    for line, value in enumerate(values):
        bar_ref[pl.ds(line, blocks, stride=ROWS), :] = value
    scatter(bar_ref, devices, ta_ref, tb_ref, blocks, acc_ref)

    def feature(line):
        if line == SCALAR:
            return jnp.broadcast_to(scalar, (devices, LANES))
        return acc_ref[pl.ds(line, devices, stride=ROWS), :]

    pack(feature, out_ref, devices, slots)


def call(body, outs, scratch, name, *args):
    return pl.pallas_call(
        body,
        out_shape=[jax.ShapeDtypeStruct(shape, F32) for shape in outs],
        scratch_shapes=[pltpu.VMEM(shape, dtype) for shape, dtype in scratch],
        compiler_params=pltpu.CompilerParams(vmem_limit_bytes=VMEM_LIMIT),
        name=name,
    )(*args)


VMEM_LIMIT = 40 * 1024 * 1024


def local(attributes, tile_anchor, target, preconditioner, send_index, tile_list, pair_index):
    view_count = lax.axis_size("view")
    devices = lax.axis_size("cell") * view_count
    slots = send_index.shape[2]
    gaussians = attributes.shape[1]
    tiles = tile_list.shape[0]
    chunks, blocks = gaussians // LANES, tiles * KSLOTS // LANES
    depth = payload_rows(slots)

    ids = jnp.pad(send_index[0], ((0, 0), (0, LANES - slots)), constant_values=-1)
    sa, sb = ids >> 7, jnp.where(ids < 0, -1, ids & (LANES - 1))
    entries = tile_list.reshape(blocks, LANES)
    ta, tb = entries // slots, entries % slots
    anchors = jnp.broadcast_to(tile_anchor[:, :, None], (2, tiles, KSLOTS)).reshape(2, blocks, LANES)
    ax, ay = anchors[0], anchors[1]
    pair_row, pair_column = pair_index.reshape(1, tiles), pair_index.reshape(tiles, 1)

    owner_meta = (chunks, devices, slots)
    tile_meta = (blocks, devices, slots)
    payload = (devices * depth, LANES)
    field = (blocks, PIXELS, LANES)
    owned = (ATTRS, gaussians)
    images, maps, scalars = (blocks * ROWS, PIXELS), (tiles, PIXELS), (16, LANES)
    chunked = ((chunks * ROWS, LANES), F32)
    arrived = ((devices * ROWS, LANES), F32)
    listed = ((blocks * ROWS, LANES), F32)
    terms = ((blocks * 32, LANES), F32)

    def exchange(value):
        value = value.reshape(devices, 1, depth * LANES)
        value = lax.all_to_all(value, ("cell", "view"), split_axis=0, concat_axis=0, tiled=True)
        return value.reshape(payload)

    def shifted(value, by):
        return lax.ppermute(value, "view", [(i, (i + by) % view_count) for i in range(view_count)])

    def owner_scratch(parts):
        return [chunked, chunked, ((chunks * ROWS, parts * LANES), BF16), arrived]

    def tile_scratch(parts):
        return [arrived, ((devices * ROWS, parts * LANES), BF16), terms]

    def pull(mode, image, maps_here, extra, outs):
        here, ordered = maps_here
        return call(
            functools.partial(tile_pull, tile_meta, mode),
            [payload] + outs,
            [(maps, F32), listed, listed, arrived],
            "pull",
            image, here, shifted(here, -1), shifted(ordered, 1), pair_column, ta, tb, ax, ay, theta, weight, rho, *extra,
        )

    (sent,) = call(functools.partial(first_owner, owner_meta), [payload], owner_scratch(3), "project", attributes, sa, sb)
    theta, weight, rho, image, here, ordered = call(
        functools.partial(tile_forward, tile_meta),
        [listed[0], field, field, images, maps, maps],
        tile_scratch(3),
        "forward",
        exchange(sent), ta, tb, ax, ay, target, pair_row,
    )
    (sent,) = pull(0, image, (here, ordered), (), [])
    sent, residual, direction = call(
        functools.partial(owner_step, owner_meta, True),
        [payload, owned, owned],
        owner_scratch(2) + [chunked, chunked, chunked],
        "gradient",
        exchange(sent), attributes, preconditioner, sa, sb,
    )
    image, here, ordered, first_sums = call(
        functools.partial(tile_tangent, tile_meta, True),
        [images, maps, maps, scalars],
        tile_scratch(2) + [listed],
        "tangent",
        exchange(sent), ta, tb, ax, ay, pair_row, theta, weight, rho,
    )
    (sent,) = pull(1, image, (here, ordered), (direction,), [])
    sent, residual, update, scaled = call(
        functools.partial(owner_step, owner_meta, False),
        [payload, owned, owned, owned],
        owner_scratch(2) + [chunked, chunked, chunked],
        "step",
        exchange(sent), attributes, preconditioner, sa, sb, residual, direction, first_sums,
    )
    image, here, ordered, sums = call(
        functools.partial(tile_tangent, tile_meta, False),
        [images, maps, maps, scalars],
        tile_scratch(2) + [listed],
        "tangent_next",
        exchange(sent), ta, tb, ax, ay, pair_row, theta, weight, rho, image, here, first_sums,
    )
    sent, direction = pull(2, image, (here, ordered), (scaled, direction, sums), [owned])
    update, residual = call(
        functools.partial(last_owner, owner_meta),
        [owned, owned],
        [chunked, arrived, chunked, chunked],
        "finish",
        exchange(sent), attributes, sa, sb, residual, update, direction, sums,
    )
    return (update, residual)


def solution(mesh):
    in_specs = (
        P(None, ("cell", "view")),
        P(None, ("cell", "view")),
        P(("cell", "view"), None, None),
        P(None, None, ("cell", "view")),
        P(("cell", "view"), None, None),
        P(("cell", "view"), None),
        P(("cell", "view")),
    )
    out_specs = (P(None, ("cell", "view")), P(None, ("cell", "view")))
    return jax.shard_map(local, mesh=mesh, in_specs=in_specs, out_specs=out_specs, check_vma=False)
```

```python
import functools
import math

import jax
import jax.numpy as jnp
from jax import lax
from jax.experimental import pallas as pl
from jax.experimental.pallas import tpu as pltpu
from jax.sharding import PartitionSpec as P

ITERS = 2
DAMPING = 0.5
PRIOR_WEIGHT = 0.3
DILATION = 0.3

F32 = jnp.float32
BF16 = jnp.bfloat16
LANES = 128
ROWS = 16
SCALAR = 6
ACTIVE = (0, 1, 2, 3, 4, 5, 6, 8, 9, 10, 11, 12)
KSLOTS = 64
PIXELS = 256
WIDE = 2 * LANES
TOGETHER = 4
ATTRS = 14


def camera_axes():
    tilt_cos, tilt_sin = (math.cos(0.3), math.sin(0.3))
    turn_cos, turn_sin = (math.cos(0.2), math.sin(0.2))
    return (
        (turn_cos, turn_sin * tilt_sin, turn_sin * tilt_cos),
        (0.0, tilt_cos, -tilt_sin),
        (-turn_sin, turn_cos * tilt_sin, turn_cos * tilt_cos),
    )


CAM = camera_axes()


def payload_rows(slots):
    return -(-len(ACTIVE) * slots // LANES)


def iota(shape, dim):
    return lax.broadcasted_iota(jnp.int32, shape, dim)


def split(value, parts):
    pieces = []
    for _ in range(parts - 1):
        piece = value.astype(BF16)
        pieces.append(piece)
        value = value - piece.astype(F32)
    pieces.append(value.astype(BF16))
    return pieces


def dot(a, b):
    return jnp.dot(a, b, preferred_element_type=F32)


def dot_nt(a, b):
    return lax.dot_general(a, b, (((1,), (1,)), ((), ())), preferred_element_type=F32)


def total(value):
    return jnp.sum(jnp.sum(value, axis=0, keepdims=True), axis=1, keepdims=True)


def pack(feature, out_ref, count, slots):
    depth = payload_rows(slots)
    lane = iota((count, LANES), 1)
    rows = [jnp.zeros((count, LANES), F32) for _ in range(depth)]
    for place, row in enumerate(ACTIVE):
        value = feature(row)
        at, offset = divmod(place * slots, LANES)
        end = offset + slots
        if offset:
            value = pltpu.roll(value, offset, 1)
        rows[at] = jnp.where((lane >= offset) & (lane < end), value, rows[at])
        if end > LANES:
            rows[at + 1] = jnp.where(lane < end - LANES, value, rows[at + 1])
    for at in range(depth):
        out_ref[pl.ds(at, count, stride=depth), :] = rows[at]


def unpack(in_ref, count, slots):
    depth = payload_rows(slots)
    lane = iota((count, LANES), 1)
    rows = [in_ref[pl.ds(at, count, stride=depth), :] for at in range(depth)]
    features = {}
    for place, row in enumerate(ACTIVE):
        at, offset = divmod(place * slots, LANES)
        value = rows[at]
        if offset + slots > LANES:
            value = jnp.where(lane >= offset, value, rows[at + 1])
        if offset:
            value = pltpu.roll(value, LANES - offset, 1)
        features[row] = jnp.where(lane < slots, value, 0.0)
    return features


def put_features(features, ref, count):
    ref[...] = jnp.zeros(ref.shape, F32)
    for row, value in features.items():
        ref[pl.ds(row, count, stride=ROWS), :] = value


def put_halves(chunk_index, lane, count, valid, a_ref, b_ref):
    half = count // 2
    upper = chunk_index >= half
    a_ref[...] = jnp.where(valid, jnp.where(upper, chunk_index - half, chunk_index), -1)
    b_ref[...] = jnp.where(valid, jnp.where(upper, LANES + lane, lane), -1)


def put_onehot(index_b, blocks, out_ref):
    wide = iota((WIDE, LANES), 0)
    for i in range(blocks):
        hit = jnp.where(wide == index_b[i : i + 1, :], 1.0, 0.0)
        out_ref[:, i * LANES : (i + 1) * LANES] = hit.astype(BF16)


def rows_of(index_ref, step):
    first = step * TOGETHER
    return jnp.concatenate([index_ref[pl.ds(first + i, 1), :] for i in range(TOGETHER)], axis=1)


def lanes_of(ref, step):
    width = TOGETHER * LANES
    return ref[:, pl.ds(pl.multiple_of(step * width, width), width)]


def gather(source_ref, chunks, index_a, onehot_ref, blocks, parts, lhs_ref, out_ref):
    half = chunks // 2
    for part, piece in enumerate(split(source_ref[...], parts)):
        for side in range(2):
            lhs_ref[:, part * WIDE + side * LANES : part * WIDE + (side + 1) * LANES] = piece[
                side * half * ROWS : (side + 1) * half * ROWS
            ]

    def body(step, carry):
        which = rows_of(index_a, step)
        onehot = lanes_of(onehot_ref, step)
        product = dot(lhs_ref[...], jnp.concatenate([onehot] * parts, axis=0))
        picked = product[:ROWS]
        for a in range(1, half):
            picked = jnp.where(which == a, product[a * ROWS : (a + 1) * ROWS], picked)
        for i in range(TOGETHER):
            start = pl.multiple_of((step * TOGETHER + i) * ROWS, ROWS)
            out_ref[pl.ds(start, ROWS), :] = picked[:, i * LANES : (i + 1) * LANES]
        return carry

    lax.fori_loop(0, blocks // TOGETHER, body, 0, unroll=2)


def scatter(source_ref, chunks, index_a, onehot_ref, blocks, acc_ref):
    half = chunks // 2
    acc_ref[...] = jnp.zeros(acc_ref.shape, F32)

    def body(step, carry):
        left = [[], []]
        for i in range(TOGETHER):
            at = step * TOGETHER + i
            value = source_ref[pl.ds(pl.multiple_of(at * ROWS, ROWS), ROWS), :]
            which = jnp.broadcast_to(index_a[pl.ds(at, 1), :], (ROWS, LANES)).astype(F32).astype(BF16)
            masks = [which == jnp.asarray(a, BF16) for a in range(half)]
            for part, piece in enumerate(split(value, 2)):
                nothing = jnp.zeros_like(piece)
                left[part].append(jnp.concatenate([jnp.where(mask, piece, nothing) for mask in masks], axis=0))
        onehot = lanes_of(onehot_ref, step)
        product = dot_nt(jnp.concatenate(left[0] + left[1], axis=1), jnp.concatenate([onehot, onehot], axis=1))
        for side in range(2):
            acc_ref[side] += column(product, side)
        return carry

    lax.fori_loop(0, blocks // TOGETHER, body, 0, unroll=2)


def wide_reader(ref, count):
    half = count // 2
    return lambda row: jnp.concatenate(
        [ref[side, pl.ds(row, half, stride=ROWS), :] for side in range(2)], axis=0
    )


def geometry(attr):
    e3, e5, e8 = jnp.exp(attr(3)), jnp.exp(attr(5)), jnp.exp(attr(8))
    a4, a6, a7, a9 = attr(4), attr(6), attr(7), attr(9)
    m = [
        (
            CAM[r][0] * e3 + CAM[r][1] * a4 + CAM[r][2] * a6,
            CAM[r][1] * e5 + CAM[r][2] * a7,
            CAM[r][2] * e8,
        )
        for r in range(2)
    ]
    sxx = m[0][0] * m[0][0] + m[0][1] * m[0][1] + m[0][2] * m[0][2] + DILATION
    sxy = m[0][0] * m[1][0] + m[0][1] * m[1][1] + m[0][2] * m[1][2]
    syy = m[1][0] * m[1][0] + m[1][1] * m[1][1] + m[1][2] * m[1][2] + DILATION
    inverse = 1.0 / (sxx * syy - sxy * sxy)
    return {
        "e": (e3, e5, e8),
        "m": m,
        "q": (syy * inverse, -sxy * inverse, sxx * inverse),
        "fade": 1.0 / (1.0 + jnp.exp(a9)),
        "a9": a9,
    }


def place(value):
    return [CAM[r][0] * value(0) + CAM[r][1] * value(1) + CAM[r][2] * value(2) for r in range(3)]


def project(attr, geo):
    x, y, z = place(attr)
    a9 = geo["a9"]
    shade = math.log(0.99) - (jnp.maximum(-a9, 0.0) + jnp.log(1.0 + jnp.exp(-jnp.abs(a9))))
    rows = {0: x, 1: y, 12: z, 2: geo["q"][0], 3: geo["q"][1], 4: geo["q"][2], 5: shade}
    for band in range(4):
        rows[8 + band] = attr(10 + band)
    return rows


def project_tangent(v, geo):
    x, y, z = place(v)
    (e3, e5, e8), m, (qxx, qxy, qyy) = geo["e"], geo["m"], geo["q"]
    v3, v5, v8 = e3 * v(3), e5 * v(5), e8 * v(8)
    d = [
        (
            CAM[r][0] * v3 + CAM[r][1] * v(4) + CAM[r][2] * v(6),
            CAM[r][1] * v5 + CAM[r][2] * v(7),
            CAM[r][2] * v8,
        )
        for r in range(2)
    ]
    sxx = 2.0 * (m[0][0] * d[0][0] + m[0][1] * d[0][1] + m[0][2] * d[0][2])
    syy = 2.0 * (m[1][0] * d[1][0] + m[1][1] * d[1][1] + m[1][2] * d[1][2])
    sxy = sum(m[0][c] * d[1][c] + d[0][c] * m[1][c] for c in range(3))
    rows = {
        0: x,
        1: y,
        12: z,
        2: -(qxx * qxx * sxx + 2.0 * qxx * qxy * sxy + qxy * qxy * syy),
        3: -(qxx * qxy * sxx + (qxx * qyy + qxy * qxy) * sxy + qxy * qyy * syy),
        4: -(qxy * qxy * sxx + 2.0 * qxy * qyy * sxy + qyy * qyy * syy),
        5: geo["fade"] * v(9),
    }
    for band in range(4):
        rows[8 + band] = v(10 + band)
    return rows


def project_cotangent(t, geo):
    (e3, e5, e8), m, (qxx, qxy, qyy) = geo["e"], geo["m"], geo["q"]
    bxx, bxy, byy = t(2), t(3), t(4)
    sxx = -(qxx * qxx * bxx + qxx * qxy * bxy + qxy * qxy * byy)
    sxy = -(2.0 * qxx * qxy * bxx + (qxx * qyy + qxy * qxy) * bxy + 2.0 * qxy * qyy * byy)
    syy = -(qxy * qxy * bxx + qxy * qyy * bxy + qyy * qyy * byy)
    n0 = [2.0 * sxx * m[0][c] + sxy * m[1][c] for c in range(3)]
    n1 = [2.0 * syy * m[1][c] + sxy * m[0][c] for c in range(3)]
    x, y, z = t(0), t(1), t(12)
    out = {j: CAM[0][j] * x + CAM[1][j] * y + CAM[2][j] * z for j in range(3)}
    out[3] = e3 * (CAM[0][0] * n0[0] + CAM[1][0] * n1[0])
    out[4] = CAM[0][1] * n0[0] + CAM[1][1] * n1[0]
    out[5] = e5 * (CAM[0][1] * n0[1] + CAM[1][1] * n1[1])
    out[6] = CAM[0][2] * n0[0] + CAM[1][2] * n1[0]
    out[7] = CAM[0][2] * n0[1] + CAM[1][2] * n1[1]
    out[8] = e8 * (CAM[0][2] * n0[2] + CAM[1][2] * n1[2])
    out[9] = geo["fade"] * t(5)
    for band in range(4):
        out[10 + band] = t(8 + band)
    return out


def to_chunks(ref, chunk_ref, chunks):
    for a in range(chunks):
        chunk_ref[a * ROWS : a * ROWS + ATTRS, :] = ref[:, a * LANES : (a + 1) * LANES]


def reader(ref, count):
    return lambda row: ref[pl.ds(row, count, stride=ROWS), :]


def chunk(ref, a):
    return ref[a * ROWS : a * ROWS + ATTRS, :]


def send_rows(rows, scalar, meta, sa_ref, so_ref, source_ref, lhs_ref, sent_ref, out_ref, parts):
    chunks, devices, slots = meta
    put_features(rows, source_ref, chunks)
    gather(source_ref, chunks, sa_ref, so_ref, devices, parts, lhs_ref, sent_ref)

    def feature(row):
        if row == SCALAR:
            return jnp.broadcast_to(scalar, (devices, LANES))
        return sent_ref[pl.ds(row, devices, stride=ROWS), :]

    pack(feature, out_ref, devices, slots)


def first_owner(
    meta, attr_ref, send_ref, out_ref, sa_ref, so_ref, chunk_ref, source_ref, lhs_ref, sent_ref, ids_ref, sb_ref
):
    chunks, devices, slots = meta
    ids_ref[...] = jnp.full(ids_ref.shape, -1, jnp.int32)
    ids_ref[:, :slots] = send_ref[...]
    ids = ids_ref[...]
    put_halves(ids >> 7, ids & (LANES - 1), chunks, ids >= 0, sa_ref, sb_ref)
    put_onehot(sb_ref, devices, so_ref)
    to_chunks(attr_ref, chunk_ref, chunks)
    attr = reader(chunk_ref, chunks)
    rows = project(attr, geometry(attr))
    send_rows(rows, jnp.zeros((1, 1), F32), meta, sa_ref, so_ref, source_ref, lhs_ref, sent_ref, out_ref, 3)


def receive_cotangent(meta, recv_ref, sa_ref, so_ref, sent_ref, acc_ref, grad_ref, geo):
    chunks, devices, slots = meta
    features = unpack(recv_ref, devices, slots)
    put_features(features, sent_ref, devices)
    scatter(sent_ref, chunks, sa_ref, so_ref, devices, acc_ref)
    for j, value in project_cotangent(wide_reader(acc_ref, chunks), geo).items():
        grad_ref[pl.ds(j, chunks, stride=ROWS), :] = value
    return features[SCALAR]


def first_lane(value):
    return total(jnp.where(iota(value.shape, 1) == 0, value, 0.0))


def apply_scaling(pre_ref, source_ref, a):
    result = None
    for i in range(ATTRS):
        term = pre_ref[i, :, a * LANES : (a + 1) * LANES] * source_ref[a * ROWS + i : a * ROWS + i + 1, :]
        result = term if result is None else result + term
    return result


def owner_step(
    meta, first, recv_ref, attr_ref, pre_ref, sa_ref, so_ref, *rest
):
    if first:
        (out_ref, res_out, dir_out, chunk_ref, source_ref, lhs_ref, sent_ref, acc_ref, grad_ref, dir_ref) = rest
    else:
        (
            res_in, dir_in, sc_ref,
            out_ref, res_out, sol_out, dir_out,
            chunk_ref, source_ref, lhs_ref, sent_ref, acc_ref, grad_ref, dir_ref,
        ) = rest
    chunks, devices, slots = meta
    to_chunks(attr_ref, chunk_ref, chunks)
    attr = reader(chunk_ref, chunks)
    geo = geometry(attr)
    scalars = receive_cotangent(meta, recv_ref, sa_ref, so_ref, sent_ref, acc_ref, grad_ref, geo)
    if not first:
        step = sc_ref[0:1, 0:1] / first_lane(scalars)
    norm = jnp.zeros((ATTRS, LANES), F32)
    for a in range(chunks):
        here = slice(a * LANES, (a + 1) * LANES)
        if first:
            residual = -chunk(grad_ref, a)
        else:
            before = dir_in[:, here]
            image = chunk(grad_ref, a) + DAMPING * before
            residual = res_in[:, here] - step * image
            sol_out[:, here] = step * before
        res_out[:, here] = residual
        grad_ref[a * ROWS : a * ROWS + ATTRS, :] = residual
        scaled = apply_scaling(pre_ref, grad_ref, a)
        dir_out[:, here] = scaled
        dir_ref[a * ROWS : a * ROWS + ATTRS, :] = scaled
        norm = norm + residual * scaled
    rows = project_tangent(reader(dir_ref, chunks), geo)
    send_rows(rows, total(norm), meta, sa_ref, so_ref, source_ref, lhs_ref, sent_ref, out_ref, 2)


def last_owner(
    meta, recv_ref, attr_ref, sa_ref, so_ref, res_in, sol_in, dir_in, sc_ref,
    sol_out, res_out, chunk_ref, sent_ref, acc_ref, grad_ref,
):
    chunks, devices, slots = meta
    to_chunks(attr_ref, chunk_ref, chunks)
    geo = geometry(reader(chunk_ref, chunks))
    scalars = receive_cotangent(meta, recv_ref, sa_ref, so_ref, sent_ref, acc_ref, grad_ref, geo)
    step = sc_ref[0:1, 0:1] / first_lane(scalars)
    for a in range(chunks):
        here = slice(a * LANES, (a + 1) * LANES)
        direction = dir_in[:, here]
        image = chunk(grad_ref, a) + DAMPING * direction
        sol_out[:, here] = sol_in[:, here] + step * direction
        res_out[:, here] = res_in[:, here] - step * image


def pixel_basis(shape, pixel_dim, term_dim):
    pixel, term = iota(shape, pixel_dim), iota(shape, term_dim) & 7
    x = (pixel & 15).astype(F32) - 7.5
    y = (pixel >> 4).astype(F32) - 7.5
    value = jnp.zeros(shape, F32)
    for m, field in enumerate((jnp.ones(shape, F32), x, y, x * x, x * y, y * y)):
        value = jnp.where(term == m, field, value)
    return value


def triangle(rows, later):
    shape = (rows, LANES)
    row, column = iota(shape, 0) & (LANES - 1), iota(shape, 1)
    same = (row >> 6) == (column >> 6)
    order = (row > column) if later else (row < column)
    return jnp.where(same & order, 1.0, 0.0).astype(BF16)


def put_terms(terms, ref, blocks):
    ref[...] = jnp.zeros(ref.shape, F32)
    for m, term in enumerate(terms):
        for part, piece in enumerate(split(term, 3)):
            ref[pl.ds(part * 8 + m, blocks, stride=32), :] = piece.astype(F32)


def tables(
    meta, list_ref, anchor_ref, ta_ref, ax_ref, ay_ref, onehot_ref, basis_ref, moment_ref, early_ref, late_ref,
    wide_ref, tb_ref,
):
    blocks, devices, slots = meta
    wide_ref[:, :KSLOTS] = list_ref[...]
    even, odd = (wide_ref[pl.ds(side, blocks, stride=2), :] for side in range(2))
    lane = iota((blocks, LANES), 1)
    entries = jnp.where(lane < KSLOTS, even, pltpu.roll(odd, KSLOTS, 1))
    source = ((entries.astype(F32) + 0.5) * (1.0 / slots)).astype(jnp.int32)
    put_halves(source, entries - slots * source, devices, entries >= 0, ta_ref, tb_ref)
    put_onehot(tb_ref, blocks, onehot_ref)
    tile, block = iota((blocks, 2 * blocks), 1), iota((blocks, 2 * blocks), 0)
    for axis, ref in enumerate((ax_ref, ay_ref)):
        sides = [
            jnp.sum(jnp.where(tile == 2 * block + side, anchor_ref[axis : axis + 1, :], 0.0), axis=1, keepdims=True)
            for side in range(2)
        ]
        ref[...] = jnp.where(lane < KSLOTS, sides[0], sides[1])
    basis = pixel_basis((PIXELS, 32), 0, 1)
    basis_ref[...] = jnp.where(iota((PIXELS, 32), 1) < 24, basis, 0.0).astype(BF16)
    moments = pixel_basis((ROWS, PIXELS), 1, 0)
    moments = jnp.where(iota((ROWS, PIXELS), 0) < 8, moments, 0.0).astype(BF16)
    moment_ref[...] = jnp.concatenate([moments, moments], axis=1)
    early_ref[...] = triangle(3 * LANES, False)
    late_ref[...] = triangle(2 * LANES, True)


def two_tiles(value):
    low = iota((8, LANES), 1) < KSLOTS
    return jnp.concatenate([jnp.where(low, value, 0.0), jnp.where(low, 0.0, value)], axis=0)


def stacked_lhs(value):
    high, low = split(value, 2)
    return jnp.concatenate(
        [jnp.concatenate([high, high], axis=1), jnp.concatenate([low, jnp.zeros_like(low)], axis=1)], axis=0
    )


def fold(value):
    half = value.shape[0] // 2
    return value[:half] + value[half:]


def side_by_side(value, parts):
    return jnp.concatenate(split(value, parts), axis=1)


def local_place(theta, ax_ref, ay_ref):
    return theta(0) - ax_ref[...] - 8.0, theta(1) - ay_ref[...] - 8.0


def send_order(pr_ref, depth, ds_ref):
    tiles = depth.shape[0]
    onehot = jnp.where(iota((tiles, tiles), 0) == pr_ref[...], 1.0, 0.0).astype(BF16)
    ds_ref[...] = sum(dot(onehot, piece) for piece in split(depth, 3))


def receive_rows(meta, recv_ref, ta_ref, to_ref, source_ref, lhs_ref, out_ref, parts):
    blocks, devices, slots = meta
    features = unpack(recv_ref, devices, slots)
    put_features(features, source_ref, devices)
    gather(source_ref, devices, ta_ref, to_ref, blocks, parts, lhs_ref, out_ref)
    return features[SCALAR]


def coefficients(term_ref, first):
    return jnp.concatenate(
        [
            term_ref[pl.ds(pl.multiple_of((first + i) * 32, 32), 32), :].astype(BF16)
            for i in range(TOGETHER)
        ],
        axis=1,
    )


def column(value, i):
    return value[:, i * LANES : (i + 1) * LANES]


def row_block(value, i):
    return value[i * PIXELS : (i + 1) * PIXELS]


def starts(first):
    return [pl.multiple_of((first + i) * ROWS, ROWS) for i in range(TOGETHER)]


def tile_forward(
    meta, recv_ref, ta_ref, to_ref, basis_ref, early_ref, ax_ref, ay_ref, target_ref, pr_ref,
    theta_ref, w_ref, ws_ref, rho_ref, left_ref, j_ref, d_ref, ds_ref,
    source_ref, lhs_ref, term_ref,
):
    blocks, devices, slots = meta
    receive_rows(meta, recv_ref, ta_ref, to_ref, source_ref, lhs_ref, theta_ref, 3)
    theta = reader(theta_ref, blocks)
    dx, dy = local_place(theta, ax_ref, ay_ref)
    qxx, qxy, qyy = theta(2), theta(3), theta(4)
    gx, gy = qxx * dx + qxy * dy, qxy * dx + qyy * dy
    terms = (theta(5) - 0.5 * (dx * gx + dy * gy), gx, gy, -0.5 * qxx, -qxy, -0.5 * qyy)
    put_terms(terms, term_ref, blocks)

    def body(step, carry):
        first = step * TOGETHER
        each = range(TOGETHER)
        product = dot(basis_ref[...], coefficients(term_ref, first))
        exponents = [column(product, i) for i in each]
        coverages = [jnp.exp(value) for value in exponents]
        logs = [jnp.log(1.0 - value) for value in coverages]
        for i in each:
            rho_ref[first + i] = jnp.exp(exponents[i] - logs[i])
        before = dot(jnp.concatenate([side_by_side(value, 3) for value in logs], axis=0), early_ref[...])
        lefts = []
        for i, start in enumerate(starts(first)):
            left = stacked_lhs(two_tiles(theta_ref[pl.ds(start + 8, 8), :]))
            left_ref[pl.ds(pl.multiple_of((first + i) * 32, 32), 32), :] = left
            lefts.append(left)
        images = []
        for i in each:
            weight = jnp.exp(row_block(before, i)) * coverages[i]
            w_ref[first + i] = weight
            pieces = side_by_side(weight, 2)
            ws_ref[first + i] = pieces
            images.append(fold(dot_nt(lefts[i], pieces)))
        for i, start in enumerate(starts(first)):
            image = images[i]
            j_ref[pl.ds(start, ROWS), :] = image
            j_ref[pl.ds(start, 4), :] = image[0:4] - target_ref[2 * (first + i)]
            j_ref[pl.ds(start + 8, 4), :] = image[8:12] - target_ref[2 * (first + i) + 1]
            d_ref[pl.ds(2 * (first + i), 1), :] = image[4:5]
            d_ref[pl.ds(2 * (first + i) + 1, 1), :] = image[12:13]
        return carry

    lax.fori_loop(0, blocks // TOGETHER, body, 0)
    send_order(pr_ref, d_ref[...], ds_ref)


def tile_tangent(
    meta, first_time, recv_ref, ta_ref, to_ref, basis_ref, early_ref, ax_ref, ay_ref, pr_ref,
    theta_ref, w_ref, ws_ref, rho_ref, left_ref, *rest
):
    if first_time:
        j_ref, d_ref, ds_ref, sc_ref, source_ref, lhs_ref, term_ref, dot_ref = rest
    else:
        j_in, sc_in, j_ref, d_ref, ds_ref, sc_ref, source_ref, lhs_ref, term_ref, dot_ref = rest
    blocks, devices, slots = meta
    norm = first_lane(receive_rows(meta, recv_ref, ta_ref, to_ref, source_ref, lhs_ref, dot_ref, 2))
    if not first_time:
        ratio = norm / sc_in[0:1, 0:1]
        sc_ref[8:16, :] = jnp.broadcast_to(ratio, (8, LANES))
    else:
        sc_ref[8:16, :] = jnp.zeros((8, LANES), F32)
    sc_ref[0:8, :] = jnp.broadcast_to(norm, (8, LANES))
    theta, tangent = reader(theta_ref, blocks), reader(dot_ref, blocks)
    dx, dy = local_place(theta, ax_ref, ay_ref)
    qxx, qxy, qyy = theta(2), theta(3), theta(4)
    gx, gy = qxx * dx + qxy * dy, qxy * dx + qyy * dy
    tx, ty, txx, txy, tyy = (tangent(row) for row in range(5))
    hx = txx * dx + txy * dy + qxx * tx + qxy * ty
    hy = txy * dx + tyy * dy + qxy * tx + qyy * ty
    constant = tangent(5) - 0.5 * (tx * gx + dx * hx + ty * gy + dy * hy)
    put_terms((constant, hx, hy, -0.5 * txx, -txy, -0.5 * tyy), term_ref, blocks)

    def body(step, carry):
        first = step * TOGETHER
        each = range(TOGETHER)
        product = dot(basis_ref[...], coefficients(term_ref, first))
        changes = [column(product, i) for i in each]
        scaled = [side_by_side(rho_ref[first + i] * changes[i], 2) for i in each]
        before = dot(jnp.concatenate(scaled, axis=0), early_ref[: 2 * LANES, :])
        images = []
        for i, start in enumerate(starts(first)):
            change = w_ref[first + i] * (changes[i] - row_block(before, i))
            left = left_ref[pl.ds(pl.multiple_of((first + i) * 32, 32), 32), :]
            left_change = stacked_lhs(two_tiles(dot_ref[pl.ds(start + 8, 8), :]))
            images.append(
                fold(
                    dot_nt(
                        jnp.concatenate([left, left_change], axis=1),
                        jnp.concatenate([side_by_side(change, 2), ws_ref[first + i]], axis=1),
                    )
                )
            )
        for i, start in enumerate(starts(first)):
            image = images[i]
            if not first_time:
                image = image + ratio * j_in[pl.ds(start, ROWS), :]
            j_ref[pl.ds(start, ROWS), :] = image
            d_ref[pl.ds(2 * (first + i), 1), :] = image[4:5]
            d_ref[pl.ds(2 * (first + i) + 1, 1), :] = image[12:13]
        return carry

    lax.fori_loop(0, blocks // TOGETHER, body, 0)
    send_order(pr_ref, d_ref[...], ds_ref)


def tile_pull(
    meta, mode, j_ref, d_ref, next_ref, past_ref, pr_ref, ta_ref, to_ref, moment_ref, late_ref, ax_ref, ay_ref,
    theta_ref, w_ref, ws_ref, rho_ref, left_ref, *rest
):
    if mode == 0:
        out_ref, cot_ref, turned_ref, term_ref, bar_ref, acc_ref = rest
    elif mode == 1:
        dir_in, out_ref, cot_ref, turned_ref, term_ref, bar_ref, acc_ref = rest
    else:
        scaled_in, dir_in, sc_ref, out_ref, dir_out, cot_ref, turned_ref, term_ref, bar_ref, acc_ref = rest
    blocks, devices, slots = meta
    tiles = 2 * blocks
    depth = d_ref[...]
    onehot = jnp.where(iota((tiles, tiles), 0) == pr_ref[...], 1.0, 0.0).T.astype(BF16)
    partner = sum(dot(onehot, piece) for piece in split(next_ref[...], 3))
    prior = PRIOR_WEIGHT * (depth - partner)
    depth_bar = PRIOR_WEIGHT * prior - PRIOR_WEIGHT * (PRIOR_WEIGHT * (past_ref[...] - depth))
    image = j_ref[...]
    cot_ref[...] = image
    for tile in range(tiles):
        cot_ref[tile * 8 + 4 : tile * 8 + 5, :] = depth_bar[tile : tile + 1, :]
    scalar = jnp.zeros((1, 1), F32)
    if mode:
        if mode == 1:
            direction = dir_in[...]
        else:
            direction = scaled_in[...] + sc_ref[8:9, 0:1] * dir_in[...]
            dir_out[...] = direction
        energy = jnp.where((iota(image.shape, 0) & 7) < 4, image * image, 0.0)
        scalar = total(energy) + total(prior * prior) + DAMPING * total(direction * direction)
    span = TOGETHER * ROWS
    for step in range(blocks // TOGETHER):
        high, low = split(cot_ref[step * span : (step + 1) * span, :], 2)
        high, low = high.astype(F32), low.astype(F32)
        turned_ref[step] = jnp.concatenate([high, low, high, jnp.zeros_like(high)], axis=0).T.astype(BF16)
    low_lanes = iota((8, LANES), 1) < KSLOTS

    def body(step, carry):
        first = step * TOGETHER
        each = range(TOGETHER)
        nothing = jnp.zeros((ROWS, LANES), BF16)
        columns = []
        for i in each:
            left = left_ref[pl.ds(pl.multiple_of((first + i) * 32, 32), 32), :]
            pieces = (left[:ROWS, :LANES], left[:ROWS, :LANES], left[ROWS:, :LANES], nothing)
            columns.append(
                jnp.concatenate([piece if other == i else nothing for piece in pieces for other in each], axis=0)
            )
        pulled = dot(turned_ref[step], jnp.concatenate(columns, axis=1))
        shares = [w_ref[first + i] * column(pulled, i) for i in each]
        after = dot(jnp.concatenate([side_by_side(share, 2) for share in shares], axis=0), late_ref[...])
        bars = [shares[i] - rho_ref[first + i] * row_block(after, i) for i in each]
        moments = dot(
            moment_ref[...],
            jnp.concatenate([jnp.concatenate(split(bar, 2), axis=0) for bar in bars], axis=1),
        )
        for i, start in enumerate(starts(first)):
            cot_high, cot_low = split(cot_ref[pl.ds(start, ROWS), :], 2)
            left = jnp.concatenate(
                [
                    jnp.concatenate([cot_high, cot_high], axis=1),
                    jnp.concatenate([cot_low, jnp.zeros_like(cot_low)], axis=1),
                ],
                axis=0,
            )
            pieces = ws_ref[first + i]
            colour_bar = fold(dot(left, jnp.concatenate([pieces[:, :LANES], pieces[:, LANES:]], axis=0)))
            bar_ref[pl.ds(start + 8, 8), :] = jnp.where(low_lanes, colour_bar[0:8], colour_bar[8:16])
            term_ref[pl.ds(start, 8), :] = column(moments, i)[0:8]
        return carry

    lax.fori_loop(0, blocks // TOGETHER, body, 0)
    theta, bars = reader(theta_ref, blocks), reader(term_ref, blocks)
    dx, dy = local_place(theta, ax_ref, ay_ref)
    qxx, qxy, qyy = theta(2), theta(3), theta(4)
    gx, gy = qxx * dx + qxy * dy, qxy * dx + qyy * dy
    b0 = bars(0)
    hx, hy = bars(1) - 0.5 * dx * b0, bars(2) - 0.5 * dy * b0
    values = (
        -0.5 * gx * b0 + qxx * hx + qxy * hy,
        -0.5 * gy * b0 + qxy * hx + qyy * hy,
        dx * hx - 0.5 * bars(3),
        dy * hx + dx * hy - bars(4),
        dy * hy - 0.5 * bars(5),
        b0,
        jnp.zeros_like(b0),
        jnp.zeros_like(b0),
    )
    for line, value in enumerate(values):
        bar_ref[pl.ds(line, blocks, stride=ROWS), :] = value
    scatter(bar_ref, devices, ta_ref, to_ref, blocks, acc_ref)
    summed = wide_reader(acc_ref, devices)

    def feature(line):
        if line == SCALAR:
            return jnp.broadcast_to(scalar, (devices, LANES))
        return summed(line)

    pack(feature, out_ref, devices, slots)


def call(body, outs, scratch, name, *args):
    return pl.pallas_call(
        body,
        out_shape=[jax.ShapeDtypeStruct(shape, dtype) for shape, dtype in outs],
        scratch_shapes=[pltpu.VMEM(shape, dtype) for shape, dtype in scratch],
        compiler_params=pltpu.CompilerParams(vmem_limit_bytes=VMEM_LIMIT),
        name=name,
    )(*args)


VMEM_LIMIT = 40 * 1024 * 1024


def local(attributes, tile_anchor, target, preconditioner, send_index, tile_list, pair_index):
    view_count = lax.axis_size("view")
    devices = lax.axis_size("cell") * view_count
    slots = send_index.shape[2]
    gaussians = attributes.shape[1]
    tiles = tile_list.shape[0]
    chunks, blocks = gaussians // LANES, tiles * KSLOTS // LANES
    depth = payload_rows(slots)

    pair_row = pair_index.reshape(1, tiles)

    owner_meta = (chunks, devices, slots)
    tile_meta = (blocks, devices, slots)
    shape = (devices * depth, LANES)
    payload = (shape, F32)
    field = ((blocks, PIXELS, LANES), F32)
    owned = ((ATTRS, gaussians), F32)
    images, maps, scalars = ((blocks * ROWS, PIXELS), F32), ((tiles, PIXELS), F32), ((16, LANES), F32)
    chunked = ((chunks * ROWS, LANES), F32)
    summed = ((2, chunks // 2 * ROWS, LANES), F32)
    arrived = ((devices * ROWS, LANES), F32)
    listed = ((blocks * ROWS, LANES), F32)
    terms = ((blocks * 32, LANES), F32)

    def exchange(value):
        value = value.reshape(devices, 1, depth * LANES)
        value = lax.all_to_all(value, ("cell", "view"), split_axis=0, concat_axis=0, tiled=True)
        return value.reshape(shape)

    def shifted(value, by):
        return lax.ppermute(value, "view", [(i, (i + by) % view_count) for i in range(view_count)])

    def owner_scratch(parts):
        return [chunked, chunked, ((chunks // 2 * ROWS, parts * WIDE), BF16), arrived]

    def tile_scratch(parts):
        return [arrived, ((devices // 2 * ROWS, parts * WIDE), BF16), terms]

    def pull(mode, image, maps_here, extra, outs):
        here, ordered = maps_here
        return call(
            functools.partial(tile_pull, tile_meta, mode),
            [payload] + outs,
            [
                images,
                ((blocks // TOGETHER, PIXELS, 4 * TOGETHER * ROWS), BF16),
                listed,
                listed,
                ((2, devices // 2 * ROWS, LANES), F32),
            ],
            "pull",
            image, here, shifted(here, -1), shifted(ordered, 1), pair_row, ta, onehot, moments, late, ax, ay,
            theta, weight, pieces, rho, left, *extra,
        )

    indices = ((devices, LANES), jnp.int32)
    sent, sa, sends = call(
        functools.partial(first_owner, owner_meta),
        [payload, indices, ((WIDE, devices * LANES), BF16)],
        owner_scratch(3) + [indices, indices],
        "project",
        attributes, send_index[0],
    )
    listing = ((blocks, LANES), jnp.int32)
    ta, ax, ay, onehot, basis, moments, early, late = call(
        functools.partial(tables, tile_meta),
        [
            listing,
            ((blocks, LANES), F32),
            ((blocks, LANES), F32),
            ((WIDE, blocks * LANES), BF16),
            ((PIXELS, 32), BF16),
            ((ROWS, 2 * PIXELS), BF16),
            ((3 * LANES, LANES), BF16),
            ((2 * LANES, LANES), BF16),
        ],
        [((tiles, LANES), jnp.int32), listing],
        "tables",
        tile_list, tile_anchor,
    )
    theta, weight, pieces, rho, left, image, here, ordered = call(
        functools.partial(tile_forward, tile_meta),
        [listed, field, ((blocks, PIXELS, WIDE), BF16), field, ((blocks * 32, WIDE), BF16), images, maps, maps],
        tile_scratch(3),
        "forward",
        exchange(sent), ta, onehot, basis, early, ax, ay, target, pair_row,
    )
    (sent,) = pull(0, image, (here, ordered), (), [])
    sent, residual, direction = call(
        functools.partial(owner_step, owner_meta, True),
        [payload, owned, owned],
        owner_scratch(2) + [summed, chunked, chunked],
        "gradient",
        exchange(sent), attributes, preconditioner, sa, sends,
    )
    image, here, ordered, first_sums = call(
        functools.partial(tile_tangent, tile_meta, True),
        [images, maps, maps, scalars],
        tile_scratch(2) + [listed],
        "tangent",
        exchange(sent), ta, onehot, basis, early, ax, ay, pair_row, theta, weight, pieces, rho, left,
    )
    (sent,) = pull(1, image, (here, ordered), (direction,), [])
    sent, residual, update, scaled = call(
        functools.partial(owner_step, owner_meta, False),
        [payload, owned, owned, owned],
        owner_scratch(2) + [summed, chunked, chunked],
        "step",
        exchange(sent), attributes, preconditioner, sa, sends, residual, direction, first_sums,
    )
    image, here, ordered, sums = call(
        functools.partial(tile_tangent, tile_meta, False),
        [images, maps, maps, scalars],
        tile_scratch(2) + [listed],
        "tangent_next",
        exchange(sent), ta, onehot, basis, early, ax, ay, pair_row, theta, weight, pieces, rho, left, image, first_sums,
    )
    sent, direction = pull(2, image, (here, ordered), (scaled, direction, sums), [owned])
    update, residual = call(
        functools.partial(last_owner, owner_meta),
        [owned, owned],
        [chunked, arrived, summed, chunked],
        "finish",
        exchange(sent), attributes, sa, sends, residual, update, direction, sums,
    )
    return (update, residual)


def solution(mesh):
    in_specs = (
        P(None, ("cell", "view")),
        P(None, ("cell", "view")),
        P(("cell", "view"), None, None),
        P(None, None, ("cell", "view")),
        P(("cell", "view"), None, None),
        P(("cell", "view"), None),
        P(("cell", "view")),
    )
    out_specs = (P(None, ("cell", "view")), P(None, ("cell", "view")))
    return jax.shard_map(local, mesh=mesh, in_specs=in_specs, out_specs=out_specs, check_vma=False)
```

```python
import functools
import math

import jax
import jax.numpy as jnp
from jax import lax
from jax.experimental import pallas as pl
from jax.experimental.pallas import tpu as pltpu
from jax.sharding import PartitionSpec as P

ITERS = 2
DAMPING = 0.5
PRIOR_WEIGHT = 0.3
DILATION = 0.3

F32 = jnp.float32
BF16 = jnp.bfloat16
LANES = 128
ROWS = 16
SCALAR = 6
ACTIVE = (0, 1, 2, 3, 4, 5, 6, 8, 9, 10, 11, 12)
KSLOTS = 64
PIXELS = 256
WIDE = 2 * LANES
TOGETHER = 4
GROUP = 8
ATTRS = 14


def camera_axes():
    tilt_cos, tilt_sin = (math.cos(0.3), math.sin(0.3))
    turn_cos, turn_sin = (math.cos(0.2), math.sin(0.2))
    return (
        (turn_cos, turn_sin * tilt_sin, turn_sin * tilt_cos),
        (0.0, tilt_cos, -tilt_sin),
        (-turn_sin, turn_cos * tilt_sin, turn_cos * tilt_cos),
    )


CAM = camera_axes()


def payload_rows(slots):
    return -(-len(ACTIVE) * slots // LANES)


def iota(shape, dim):
    return lax.broadcasted_iota(jnp.int32, shape, dim)


def split(value, parts):
    pieces = []
    for _ in range(parts - 1):
        piece = value.astype(BF16)
        pieces.append(piece)
        value = value - piece.astype(F32)
    pieces.append(value.astype(BF16))
    return pieces


def dot(a, b):
    return jnp.dot(a, b, preferred_element_type=F32)


def dot_nt(a, b):
    return lax.dot_general(a, b, (((1,), (1,)), ((), ())), preferred_element_type=F32)


def total(value):
    return jnp.sum(jnp.sum(value, axis=0, keepdims=True), axis=1, keepdims=True)


def pack(feature, out_ref, count, slots):
    depth = payload_rows(slots)
    lane = iota((count, LANES), 1)
    rows = [jnp.zeros((count, LANES), F32) for _ in range(depth)]
    for place, row in enumerate(ACTIVE):
        value = feature(row)
        at, offset = divmod(place * slots, LANES)
        end = offset + slots
        if offset:
            value = pltpu.roll(value, offset, 1)
        rows[at] = jnp.where((lane >= offset) & (lane < end), value, rows[at])
        if end > LANES:
            rows[at + 1] = jnp.where(lane < end - LANES, value, rows[at + 1])
    for at in range(depth):
        out_ref[pl.ds(at, count, stride=depth), :] = rows[at]


def unpack(in_ref, count, slots):
    depth = payload_rows(slots)
    lane = iota((count, LANES), 1)
    rows = [in_ref[pl.ds(at, count, stride=depth), :] for at in range(depth)]
    features = {}
    for place, row in enumerate(ACTIVE):
        at, offset = divmod(place * slots, LANES)
        value = rows[at]
        if offset + slots > LANES:
            value = jnp.where(lane >= offset, value, rows[at + 1])
        if offset:
            value = pltpu.roll(value, LANES - offset, 1)
        features[row] = jnp.where(lane < slots, value, 0.0)
    return features


def put_features(features, ref, count):
    ref[...] = jnp.zeros(ref.shape, F32)
    for row, value in features.items():
        ref[pl.ds(row, count, stride=ROWS), :] = value


def put_halves(chunk_index, lane, count, valid, a_ref, b_ref):
    half = count // 2
    upper = chunk_index >= half
    a_ref[...] = jnp.where(valid, jnp.where(upper, chunk_index - half, chunk_index), -1)
    b_ref[...] = jnp.where(valid, jnp.where(upper, LANES + lane, lane), -1)


def put_onehot(index_b, blocks, out_ref):
    wide = iota((WIDE, LANES), 0)
    for i in range(blocks):
        hit = jnp.where(wide == index_b[i : i + 1, :], 1.0, 0.0)
        out_ref[:, i * LANES : (i + 1) * LANES] = hit.astype(BF16)


def rows_of(index_ref, step):
    first = step * TOGETHER
    return jnp.concatenate([index_ref[pl.ds(first + i, 1), :] for i in range(TOGETHER)], axis=1)


def lanes_of(ref, step):
    width = TOGETHER * LANES
    return ref[:, pl.ds(pl.multiple_of(step * width, width), width)]


def whole(blocks):
    return min(blocks // TOGETHER, 8)


def gather(source_ref, chunks, index_a, onehot_ref, blocks, parts, lhs_ref, out_ref):
    half = chunks // 2
    for part, piece in enumerate(split(source_ref[...], parts)):
        for side in range(2):
            lhs_ref[:, part * WIDE + side * LANES : part * WIDE + (side + 1) * LANES] = piece[
                side * half * ROWS : (side + 1) * half * ROWS
            ]

    def body(step, carry):
        which = rows_of(index_a, step)
        onehot = lanes_of(onehot_ref, step)
        product = dot(lhs_ref[...], jnp.concatenate([onehot] * parts, axis=0))
        picked = product[:ROWS]
        for a in range(1, half):
            picked = jnp.where(which == a, product[a * ROWS : (a + 1) * ROWS], picked)
        for i in range(TOGETHER):
            start = pl.multiple_of((step * TOGETHER + i) * ROWS, ROWS)
            out_ref[pl.ds(start, ROWS), :] = picked[:, i * LANES : (i + 1) * LANES]
        return carry

    lax.fori_loop(0, blocks // TOGETHER, body, 0, unroll=whole(blocks))


def scatter(source_ref, chunks, index_a, onehot_ref, blocks, acc_ref, unroll):
    half = chunks // 2
    acc_ref[...] = jnp.zeros(acc_ref.shape, F32)

    def body(step, carry):
        left = [[], []]
        for i in range(TOGETHER):
            at = step * TOGETHER + i
            value = source_ref[pl.ds(pl.multiple_of(at * ROWS, ROWS), ROWS), :]
            which = jnp.broadcast_to(index_a[pl.ds(at, 1), :], (ROWS, LANES)).astype(F32).astype(BF16)
            masks = [which == jnp.asarray(a, BF16) for a in range(half)]
            for part, piece in enumerate(split(value, 2)):
                nothing = jnp.zeros_like(piece)
                left[part].append(jnp.concatenate([jnp.where(mask, piece, nothing) for mask in masks], axis=0))
        onehot = lanes_of(onehot_ref, step)
        product = dot_nt(jnp.concatenate(left[0] + left[1], axis=1), jnp.concatenate([onehot, onehot], axis=1))
        for side in range(2):
            acc_ref[side] += column(product, side)
        return carry

    lax.fori_loop(0, blocks // TOGETHER, body, 0, unroll=unroll)


def wide_reader(ref, count):
    half = count // 2
    return lambda row: jnp.concatenate(
        [ref[side, pl.ds(row, half, stride=ROWS), :] for side in range(2)], axis=0
    )


def geometry(attr):
    e3, e5, e8 = jnp.exp(attr(3)), jnp.exp(attr(5)), jnp.exp(attr(8))
    a4, a6, a7, a9 = attr(4), attr(6), attr(7), attr(9)
    m = [
        (
            CAM[r][0] * e3 + CAM[r][1] * a4 + CAM[r][2] * a6,
            CAM[r][1] * e5 + CAM[r][2] * a7,
            CAM[r][2] * e8,
        )
        for r in range(2)
    ]
    sxx = m[0][0] * m[0][0] + m[0][1] * m[0][1] + m[0][2] * m[0][2] + DILATION
    sxy = m[0][0] * m[1][0] + m[0][1] * m[1][1] + m[0][2] * m[1][2]
    syy = m[1][0] * m[1][0] + m[1][1] * m[1][1] + m[1][2] * m[1][2] + DILATION
    inverse = 1.0 / (sxx * syy - sxy * sxy)
    return {
        "e": (e3, e5, e8),
        "m": m,
        "q": (syy * inverse, -sxy * inverse, sxx * inverse),
        "fade": 1.0 / (1.0 + jnp.exp(a9)),
        "a9": a9,
    }


def place(value):
    return [CAM[r][0] * value(0) + CAM[r][1] * value(1) + CAM[r][2] * value(2) for r in range(3)]


def project(attr, geo):
    x, y, z = place(attr)
    a9 = geo["a9"]
    shade = math.log(0.99) - (jnp.maximum(-a9, 0.0) + jnp.log(1.0 + jnp.exp(-jnp.abs(a9))))
    rows = {0: x, 1: y, 12: z, 2: geo["q"][0], 3: geo["q"][1], 4: geo["q"][2], 5: shade}
    for band in range(4):
        rows[8 + band] = attr(10 + band)
    return rows


def project_tangent(v, geo):
    x, y, z = place(v)
    (e3, e5, e8), m, (qxx, qxy, qyy) = geo["e"], geo["m"], geo["q"]
    v3, v5, v8 = e3 * v(3), e5 * v(5), e8 * v(8)
    d = [
        (
            CAM[r][0] * v3 + CAM[r][1] * v(4) + CAM[r][2] * v(6),
            CAM[r][1] * v5 + CAM[r][2] * v(7),
            CAM[r][2] * v8,
        )
        for r in range(2)
    ]
    sxx = 2.0 * (m[0][0] * d[0][0] + m[0][1] * d[0][1] + m[0][2] * d[0][2])
    syy = 2.0 * (m[1][0] * d[1][0] + m[1][1] * d[1][1] + m[1][2] * d[1][2])
    sxy = sum(m[0][c] * d[1][c] + d[0][c] * m[1][c] for c in range(3))
    rows = {
        0: x,
        1: y,
        12: z,
        2: -(qxx * qxx * sxx + 2.0 * qxx * qxy * sxy + qxy * qxy * syy),
        3: -(qxx * qxy * sxx + (qxx * qyy + qxy * qxy) * sxy + qxy * qyy * syy),
        4: -(qxy * qxy * sxx + 2.0 * qxy * qyy * sxy + qyy * qyy * syy),
        5: geo["fade"] * v(9),
    }
    for band in range(4):
        rows[8 + band] = v(10 + band)
    return rows


def project_cotangent(t, geo):
    (e3, e5, e8), m, (qxx, qxy, qyy) = geo["e"], geo["m"], geo["q"]
    bxx, bxy, byy = t(2), t(3), t(4)
    sxx = -(qxx * qxx * bxx + qxx * qxy * bxy + qxy * qxy * byy)
    sxy = -(2.0 * qxx * qxy * bxx + (qxx * qyy + qxy * qxy) * bxy + 2.0 * qxy * qyy * byy)
    syy = -(qxy * qxy * bxx + qxy * qyy * bxy + qyy * qyy * byy)
    n0 = [2.0 * sxx * m[0][c] + sxy * m[1][c] for c in range(3)]
    n1 = [2.0 * syy * m[1][c] + sxy * m[0][c] for c in range(3)]
    x, y, z = t(0), t(1), t(12)
    out = {j: CAM[0][j] * x + CAM[1][j] * y + CAM[2][j] * z for j in range(3)}
    out[3] = e3 * (CAM[0][0] * n0[0] + CAM[1][0] * n1[0])
    out[4] = CAM[0][1] * n0[0] + CAM[1][1] * n1[0]
    out[5] = e5 * (CAM[0][1] * n0[1] + CAM[1][1] * n1[1])
    out[6] = CAM[0][2] * n0[0] + CAM[1][2] * n1[0]
    out[7] = CAM[0][2] * n0[1] + CAM[1][2] * n1[1]
    out[8] = e8 * (CAM[0][2] * n0[2] + CAM[1][2] * n1[2])
    out[9] = geo["fade"] * t(5)
    for band in range(4):
        out[10 + band] = t(8 + band)
    return out


def to_chunks(ref, chunk_ref, chunks):
    for a in range(chunks):
        chunk_ref[a * ROWS : a * ROWS + ATTRS, :] = ref[:, a * LANES : (a + 1) * LANES]


def reader(ref, count):
    return lambda row: ref[pl.ds(row, count, stride=ROWS), :]


def chunk(ref, a):
    return ref[a * ROWS : a * ROWS + ATTRS, :]


def send_rows(rows, scalar, meta, sa_ref, so_ref, source_ref, lhs_ref, sent_ref, out_ref, parts):
    chunks, devices, slots = meta
    put_features(rows, source_ref, chunks)
    gather(source_ref, chunks, sa_ref, so_ref, devices, parts, lhs_ref, sent_ref)

    def feature(row):
        if row == SCALAR:
            return jnp.broadcast_to(scalar, (devices, LANES))
        return sent_ref[pl.ds(row, devices, stride=ROWS), :]

    pack(feature, out_ref, devices, slots)


def first_owner(
    meta, attr_ref, send_ref, out_ref, sa_ref, so_ref, chunk_ref, source_ref, lhs_ref, sent_ref, ids_ref, sb_ref
):
    chunks, devices, slots = meta
    ids_ref[...] = jnp.full(ids_ref.shape, -1, jnp.int32)
    ids_ref[:, :slots] = send_ref[...]
    ids = ids_ref[...]
    put_halves(ids >> 7, ids & (LANES - 1), chunks, ids >= 0, sa_ref, sb_ref)
    put_onehot(sb_ref, devices, so_ref)
    to_chunks(attr_ref, chunk_ref, chunks)
    attr = reader(chunk_ref, chunks)
    rows = project(attr, geometry(attr))
    send_rows(rows, jnp.zeros((1, 1), F32), meta, sa_ref, so_ref, source_ref, lhs_ref, sent_ref, out_ref, 3)


def receive_cotangent(meta, recv_ref, sa_ref, so_ref, sent_ref, acc_ref, grad_ref, geo, unroll):
    chunks, devices, slots = meta
    features = unpack(recv_ref, devices, slots)
    put_features(features, sent_ref, devices)
    scatter(sent_ref, chunks, sa_ref, so_ref, devices, acc_ref, unroll)
    for j, value in project_cotangent(wide_reader(acc_ref, chunks), geo).items():
        grad_ref[pl.ds(j, chunks, stride=ROWS), :] = value
    return features[SCALAR]


def first_lane(value):
    return total(jnp.where(iota(value.shape, 1) == 0, value, 0.0))


def apply_scaling(pre_ref, source_ref, a):
    result = None
    for i in range(ATTRS):
        term = pre_ref[i, :, a * LANES : (a + 1) * LANES] * source_ref[a * ROWS + i : a * ROWS + i + 1, :]
        result = term if result is None else result + term
    return result


def owner_step(
    meta, first, recv_ref, attr_ref, pre_ref, sa_ref, so_ref, *rest
):
    if first:
        (out_ref, res_out, dir_out, chunk_ref, source_ref, lhs_ref, sent_ref, acc_ref, grad_ref, dir_ref) = rest
    else:
        (
            res_in, dir_in, sc_ref,
            out_ref, res_out, sol_out, dir_out,
            chunk_ref, source_ref, lhs_ref, sent_ref, acc_ref, grad_ref, dir_ref,
        ) = rest
    chunks, devices, slots = meta
    to_chunks(attr_ref, chunk_ref, chunks)
    attr = reader(chunk_ref, chunks)
    geo = geometry(attr)
    scalars = receive_cotangent(meta, recv_ref, sa_ref, so_ref, sent_ref, acc_ref, grad_ref, geo, 4)
    if not first:
        step = sc_ref[0:1, 0:1] / first_lane(scalars)
    norm = jnp.zeros((ATTRS, LANES), F32)
    for a in range(chunks):
        here = slice(a * LANES, (a + 1) * LANES)
        if first:
            residual = -chunk(grad_ref, a)
        else:
            before = dir_in[:, here]
            image = chunk(grad_ref, a) + DAMPING * before
            residual = res_in[:, here] - step * image
            sol_out[:, here] = step * before
        res_out[:, here] = residual
        grad_ref[a * ROWS : a * ROWS + ATTRS, :] = residual
        scaled = apply_scaling(pre_ref, grad_ref, a)
        dir_out[:, here] = scaled
        dir_ref[a * ROWS : a * ROWS + ATTRS, :] = scaled
        norm = norm + residual * scaled
    rows = project_tangent(reader(dir_ref, chunks), geo)
    send_rows(rows, total(norm), meta, sa_ref, so_ref, source_ref, lhs_ref, sent_ref, out_ref, 2)


def last_owner(
    meta, recv_ref, attr_ref, sa_ref, so_ref, res_in, sol_in, dir_in, sc_ref,
    sol_out, res_out, chunk_ref, sent_ref, acc_ref, grad_ref,
):
    chunks, devices, slots = meta
    to_chunks(attr_ref, chunk_ref, chunks)
    geo = geometry(reader(chunk_ref, chunks))
    scalars = receive_cotangent(meta, recv_ref, sa_ref, so_ref, sent_ref, acc_ref, grad_ref, geo, whole(devices))
    step = sc_ref[0:1, 0:1] / first_lane(scalars)
    for a in range(chunks):
        here = slice(a * LANES, (a + 1) * LANES)
        direction = dir_in[:, here]
        image = chunk(grad_ref, a) + DAMPING * direction
        sol_out[:, here] = sol_in[:, here] + step * direction
        res_out[:, here] = res_in[:, here] - step * image


def pixel_basis(shape, pixel_dim, term_dim):
    pixel, term = iota(shape, pixel_dim), iota(shape, term_dim) & 7
    x = (pixel & 15).astype(F32) - 7.5
    y = (pixel >> 4).astype(F32) - 7.5
    value = jnp.zeros(shape, F32)
    for m, field in enumerate((jnp.ones(shape, F32), x, y, x * x, x * y, y * y)):
        value = jnp.where(term == m, field, value)
    return value


def triangle(rows, later):
    shape = (rows, LANES)
    row, column = iota(shape, 0) & (LANES - 1), iota(shape, 1)
    same = (row >> 6) == (column >> 6)
    order = (row > column) if later else (row < column)
    return jnp.where(same & order, 1.0, 0.0).astype(BF16)


def put_terms(terms, ref, blocks):
    ref[...] = jnp.zeros(ref.shape, F32)
    for m, term in enumerate(terms):
        ref[pl.ds(m, blocks, stride=8), :] = term


def tables(
    meta, list_ref, anchor_ref, ta_ref, ax_ref, ay_ref, onehot_ref, basis_ref, moment_ref, early_ref, late_ref,
    wide_ref, tb_ref,
):
    blocks, devices, slots = meta
    wide_ref[:, :KSLOTS] = list_ref[...]
    even, odd = (wide_ref[pl.ds(side, blocks, stride=2), :] for side in range(2))
    lane = iota((blocks, LANES), 1)
    entries = jnp.where(lane < KSLOTS, even, pltpu.roll(odd, KSLOTS, 1))
    source = ((entries.astype(F32) + 0.5) * (1.0 / slots)).astype(jnp.int32)
    put_halves(source, entries - slots * source, devices, entries >= 0, ta_ref, tb_ref)
    put_onehot(tb_ref, blocks, onehot_ref)
    tile, block = iota((blocks, 2 * blocks), 1), iota((blocks, 2 * blocks), 0)
    for axis, ref in enumerate((ax_ref, ay_ref)):
        sides = [
            jnp.sum(jnp.where(tile == 2 * block + side, anchor_ref[axis : axis + 1, :], 0.0), axis=1, keepdims=True)
            for side in range(2)
        ]
        ref[...] = jnp.where(lane < KSLOTS, sides[0], sides[1])
    basis = pixel_basis((PIXELS, 32), 0, 1)
    basis_ref[...] = jnp.where(iota((PIXELS, 32), 1) < 24, basis, 0.0).astype(BF16)
    moments = pixel_basis((ROWS, PIXELS), 1, 0)
    moments = jnp.where(iota((ROWS, PIXELS), 0) < 8, moments, 0.0).astype(BF16)
    moment_ref[...] = jnp.concatenate([moments, moments], axis=1)
    early_ref[...] = triangle(3 * LANES, False)
    late_ref[...] = triangle(2 * LANES, True)


def two_tiles(value):
    low = iota((8, LANES), 1) < KSLOTS
    return jnp.concatenate([jnp.where(low, value, 0.0), jnp.where(low, 0.0, value)], axis=0)


def stacked_lhs(value):
    high, low = split(value, 2)
    return jnp.concatenate(
        [jnp.concatenate([high, high], axis=1), jnp.concatenate([low, jnp.zeros_like(low)], axis=1)], axis=0
    )


def fold(value):
    half = value.shape[0] // 2
    return value[:half] + value[half:]


def side_by_side(value, parts):
    return jnp.concatenate(split(value, parts), axis=1)


def local_place(theta, ax_ref, ay_ref):
    return theta(0) - ax_ref[...] - 8.0, theta(1) - ay_ref[...] - 8.0


def send_order(pr_ref, depth, ds_ref):
    tiles = depth.shape[0]
    onehot = jnp.where(iota((tiles, tiles), 0) == pr_ref[...], 1.0, 0.0).astype(BF16)
    ds_ref[...] = sum(dot(onehot, piece) for piece in split(depth, 3))


def receive_rows(meta, recv_ref, ta_ref, to_ref, source_ref, lhs_ref, out_ref, parts):
    blocks, devices, slots = meta
    features = unpack(recv_ref, devices, slots)
    put_features(features, source_ref, devices)
    gather(source_ref, devices, ta_ref, to_ref, blocks, parts, lhs_ref, out_ref)
    return features[SCALAR]


def coefficients(term_ref, first):
    columns = []
    for i in range(GROUP):
        value = term_ref[pl.ds(pl.multiple_of((first + i) * 8, 8), 8), :]
        pieces = [piece.astype(F32) for piece in split(value, 3)] + [jnp.zeros_like(value)]
        columns.append(jnp.concatenate(pieces, axis=0).astype(BF16))
    return jnp.concatenate(columns, axis=1)


def column(value, i):
    return value[:, i * LANES : (i + 1) * LANES]


def row_block(value, i):
    return value[i * PIXELS : (i + 1) * PIXELS]


def starts(first, count=TOGETHER):
    return [pl.multiple_of((first + i) * ROWS, ROWS) for i in range(count)]


def tile_forward(
    meta, recv_ref, ta_ref, to_ref, basis_ref, early_ref, ax_ref, ay_ref, target_ref, pr_ref,
    theta_ref, w_ref, ws_ref, rho_ref, left_ref, j_ref, d_ref, ds_ref,
    source_ref, lhs_ref, term_ref,
):
    blocks, devices, slots = meta
    receive_rows(meta, recv_ref, ta_ref, to_ref, source_ref, lhs_ref, theta_ref, 3)
    theta = reader(theta_ref, blocks)
    dx, dy = local_place(theta, ax_ref, ay_ref)
    qxx, qxy, qyy = theta(2), theta(3), theta(4)
    gx, gy = qxx * dx + qxy * dy, qxy * dx + qyy * dy
    terms = (theta(5) - 0.5 * (dx * gx + dy * gy), gx, gy, -0.5 * qxx, -qxy, -0.5 * qyy)
    put_terms(terms, term_ref, blocks)

    def body(step, carry):
        first = step * GROUP
        each = range(GROUP)
        product = dot(basis_ref[...], coefficients(term_ref, first))
        exponents = [column(product, i) for i in each]
        coverages = [jnp.exp(value) for value in exponents]
        logs = [jnp.log(1.0 - value) for value in coverages]
        for i in each:
            rho_ref[first + i] = jnp.exp(exponents[i] - logs[i])
        before = dot(jnp.concatenate([side_by_side(value, 3) for value in logs], axis=0), early_ref[...])
        lefts = []
        for i, start in enumerate(starts(first, GROUP)):
            left = stacked_lhs(two_tiles(theta_ref[pl.ds(start + 8, 8), :]))
            left_ref[pl.ds(pl.multiple_of((first + i) * 32, 32), 32), :] = left
            lefts.append(left)
        images = []
        for i in each:
            weight = jnp.exp(row_block(before, i)) * coverages[i]
            w_ref[first + i] = weight
            pieces = side_by_side(weight, 2)
            ws_ref[first + i] = pieces
            images.append(fold(dot_nt(lefts[i], pieces)))
        for i, start in enumerate(starts(first, GROUP)):
            image = images[i]
            j_ref[pl.ds(start, ROWS), :] = image
            j_ref[pl.ds(start, 4), :] = image[0:4] - target_ref[2 * (first + i)]
            j_ref[pl.ds(start + 8, 4), :] = image[8:12] - target_ref[2 * (first + i) + 1]
            d_ref[pl.ds(2 * (first + i), 1), :] = image[4:5]
            d_ref[pl.ds(2 * (first + i) + 1, 1), :] = image[12:13]
        return carry

    lax.fori_loop(0, blocks // GROUP, body, 0)
    send_order(pr_ref, d_ref[...], ds_ref)


def tile_tangent(
    meta, first_time, recv_ref, ta_ref, to_ref, basis_ref, early_ref, ax_ref, ay_ref, pr_ref,
    theta_ref, w_ref, ws_ref, rho_ref, left_ref, *rest
):
    if first_time:
        j_ref, d_ref, ds_ref, sc_ref, source_ref, lhs_ref, term_ref, dot_ref = rest
    else:
        j_in, sc_in, j_ref, d_ref, ds_ref, sc_ref, source_ref, lhs_ref, term_ref, dot_ref = rest
    blocks, devices, slots = meta
    norm = first_lane(receive_rows(meta, recv_ref, ta_ref, to_ref, source_ref, lhs_ref, dot_ref, 2))
    if not first_time:
        ratio = norm / sc_in[0:1, 0:1]
        sc_ref[8:16, :] = jnp.broadcast_to(ratio, (8, LANES))
    else:
        sc_ref[8:16, :] = jnp.zeros((8, LANES), F32)
    sc_ref[0:8, :] = jnp.broadcast_to(norm, (8, LANES))
    theta, tangent = reader(theta_ref, blocks), reader(dot_ref, blocks)
    dx, dy = local_place(theta, ax_ref, ay_ref)
    qxx, qxy, qyy = theta(2), theta(3), theta(4)
    gx, gy = qxx * dx + qxy * dy, qxy * dx + qyy * dy
    tx, ty, txx, txy, tyy = (tangent(row) for row in range(5))
    hx = txx * dx + txy * dy + qxx * tx + qxy * ty
    hy = txy * dx + tyy * dy + qxy * tx + qyy * ty
    constant = tangent(5) - 0.5 * (tx * gx + dx * hx + ty * gy + dy * hy)
    put_terms((constant, hx, hy, -0.5 * txx, -txy, -0.5 * tyy), term_ref, blocks)

    def body(step, carry):
        first = step * GROUP
        each = range(GROUP)
        product = dot(basis_ref[...], coefficients(term_ref, first))
        changes = [column(product, i) for i in each]
        scaled = [side_by_side(rho_ref[first + i] * changes[i], 2) for i in each]
        before = dot(jnp.concatenate(scaled, axis=0), early_ref[: 2 * LANES, :])
        images = []
        for i, start in enumerate(starts(first, GROUP)):
            change = w_ref[first + i] * (changes[i] - row_block(before, i))
            left = left_ref[pl.ds(pl.multiple_of((first + i) * 32, 32), 32), :]
            left_change = stacked_lhs(two_tiles(dot_ref[pl.ds(start + 8, 8), :]))
            images.append(
                fold(
                    dot_nt(
                        jnp.concatenate([left, left_change], axis=1),
                        jnp.concatenate([side_by_side(change, 2), ws_ref[first + i]], axis=1),
                    )
                )
            )
        for i, start in enumerate(starts(first, GROUP)):
            image = images[i]
            if not first_time:
                image = image + ratio * j_in[pl.ds(start, ROWS), :]
            j_ref[pl.ds(start, ROWS), :] = image
            d_ref[pl.ds(2 * (first + i), 1), :] = image[4:5]
            d_ref[pl.ds(2 * (first + i) + 1, 1), :] = image[12:13]
        return carry

    lax.fori_loop(0, blocks // GROUP, body, 0)
    send_order(pr_ref, d_ref[...], ds_ref)


def tile_pull(
    meta, mode, j_ref, d_ref, next_ref, past_ref, pr_ref, ta_ref, to_ref, moment_ref, late_ref, ax_ref, ay_ref,
    theta_ref, w_ref, ws_ref, rho_ref, left_ref, *rest
):
    if mode == 0:
        out_ref, cot_ref, turned_ref, term_ref, bar_ref, acc_ref = rest
    elif mode == 1:
        dir_in, out_ref, cot_ref, turned_ref, term_ref, bar_ref, acc_ref = rest
    else:
        scaled_in, dir_in, sc_ref, out_ref, dir_out, cot_ref, turned_ref, term_ref, bar_ref, acc_ref = rest
    blocks, devices, slots = meta
    tiles = 2 * blocks
    depth = d_ref[...]
    onehot = jnp.where(iota((tiles, tiles), 0) == pr_ref[...], 1.0, 0.0).T.astype(BF16)
    partner = sum(dot(onehot, piece) for piece in split(next_ref[...], 3))
    prior = PRIOR_WEIGHT * (depth - partner)
    depth_bar = PRIOR_WEIGHT * prior - PRIOR_WEIGHT * (PRIOR_WEIGHT * (past_ref[...] - depth))
    image = j_ref[...]
    cot_ref[...] = image
    for tile in range(tiles):
        cot_ref[tile * 8 + 4 : tile * 8 + 5, :] = depth_bar[tile : tile + 1, :]
    scalar = jnp.zeros((1, 1), F32)
    if mode:
        if mode == 1:
            direction = dir_in[...]
        else:
            direction = scaled_in[...] + sc_ref[8:9, 0:1] * dir_in[...]
            dir_out[...] = direction
        energy = jnp.where((iota(image.shape, 0) & 7) < 4, image * image, 0.0)
        scalar = total(energy) + total(prior * prior) + DAMPING * total(direction * direction)
    span = TOGETHER * ROWS
    for step in range(blocks // TOGETHER):
        high, low = split(cot_ref[step * span : (step + 1) * span, :], 2)
        turned = jnp.concatenate([high.astype(F32), low.astype(F32)], axis=0).T.astype(BF16)
        turned_ref[step] = jnp.concatenate([turned, turned], axis=1)
    low_lanes = iota((8, LANES), 1) < KSLOTS

    def body(step, carry):
        first = step * TOGETHER
        each = range(TOGETHER)
        nothing = jnp.zeros((ROWS, LANES), BF16)
        columns = []
        for i in each:
            left = left_ref[pl.ds(pl.multiple_of((first + i) * 32, 32), 32), :]
            pieces = (left[:ROWS, :LANES], left[:ROWS, :LANES], left[ROWS:, :LANES], nothing)
            columns.append(
                jnp.concatenate([piece if other == i else nothing for piece in pieces for other in each], axis=0)
            )
        pulled = dot(turned_ref[step], jnp.concatenate(columns, axis=1))
        shares = [w_ref[first + i] * column(pulled, i) for i in each]
        after = dot(jnp.concatenate([side_by_side(share, 2) for share in shares], axis=0), late_ref[...])
        bars = [shares[i] - rho_ref[first + i] * row_block(after, i) for i in each]
        moments = dot(
            moment_ref[...],
            jnp.concatenate([jnp.concatenate(split(bar, 2), axis=0) for bar in bars], axis=1),
        )
        for i, start in enumerate(starts(first)):
            cot_high, cot_low = split(cot_ref[pl.ds(start, ROWS), :], 2)
            left = jnp.concatenate(
                [
                    jnp.concatenate([cot_high, cot_high], axis=1),
                    jnp.concatenate([cot_low, jnp.zeros_like(cot_low)], axis=1),
                ],
                axis=0,
            )
            pieces = ws_ref[first + i]
            colour_bar = fold(dot(left, jnp.concatenate([pieces[:, :LANES], pieces[:, LANES:]], axis=0)))
            bar_ref[pl.ds(start + 8, 8), :] = jnp.where(low_lanes, colour_bar[0:8], colour_bar[8:16])
            term_ref[pl.ds(start, 8), :] = column(moments, i)[0:8]
        return carry

    lax.fori_loop(0, blocks // TOGETHER, body, 0, unroll=3)
    theta, bars = reader(theta_ref, blocks), reader(term_ref, blocks)
    dx, dy = local_place(theta, ax_ref, ay_ref)
    qxx, qxy, qyy = theta(2), theta(3), theta(4)
    gx, gy = qxx * dx + qxy * dy, qxy * dx + qyy * dy
    b0 = bars(0)
    hx, hy = bars(1) - 0.5 * dx * b0, bars(2) - 0.5 * dy * b0
    values = (
        -0.5 * gx * b0 + qxx * hx + qxy * hy,
        -0.5 * gy * b0 + qxy * hx + qyy * hy,
        dx * hx - 0.5 * bars(3),
        dy * hx + dx * hy - bars(4),
        dy * hy - 0.5 * bars(5),
        b0,
        jnp.zeros_like(b0),
        jnp.zeros_like(b0),
    )
    for line, value in enumerate(values):
        bar_ref[pl.ds(line, blocks, stride=ROWS), :] = value
    scatter(bar_ref, devices, ta_ref, to_ref, blocks, acc_ref, whole(blocks))
    summed = wide_reader(acc_ref, devices)

    def feature(line):
        if line == SCALAR:
            return jnp.broadcast_to(scalar, (devices, LANES))
        return summed(line)

    pack(feature, out_ref, devices, slots)


def call(body, outs, scratch, name, *args):
    return pl.pallas_call(
        body,
        out_shape=[jax.ShapeDtypeStruct(shape, dtype) for shape, dtype in outs],
        scratch_shapes=[pltpu.VMEM(shape, dtype) for shape, dtype in scratch],
        compiler_params=pltpu.CompilerParams(vmem_limit_bytes=VMEM_LIMIT),
        name=name,
    )(*args)


VMEM_LIMIT = 40 * 1024 * 1024


def local(attributes, tile_anchor, target, preconditioner, send_index, tile_list, pair_index):
    view_count = lax.axis_size("view")
    devices = lax.axis_size("cell") * view_count
    slots = send_index.shape[2]
    gaussians = attributes.shape[1]
    tiles = tile_list.shape[0]
    chunks, blocks = gaussians // LANES, tiles * KSLOTS // LANES
    depth = payload_rows(slots)

    pair_row = pair_index.reshape(1, tiles)

    owner_meta = (chunks, devices, slots)
    tile_meta = (blocks, devices, slots)
    shape = (devices * depth, LANES)
    payload = (shape, F32)
    field = ((blocks, PIXELS, LANES), F32)
    owned = ((ATTRS, gaussians), F32)
    images, maps, scalars = ((blocks * ROWS, PIXELS), F32), ((tiles, PIXELS), F32), ((16, LANES), F32)
    chunked = ((chunks * ROWS, LANES), F32)
    summed = ((2, chunks // 2 * ROWS, LANES), F32)
    arrived = ((devices * ROWS, LANES), F32)
    listed = ((blocks * ROWS, LANES), F32)
    terms = ((blocks * 8, LANES), F32)

    def exchange(value):
        value = value.reshape(devices, 1, depth * LANES)
        value = lax.all_to_all(value, ("cell", "view"), split_axis=0, concat_axis=0, tiled=True)
        return value.reshape(shape)

    def shifted(value, by):
        return lax.ppermute(value, "view", [(i, (i + by) % view_count) for i in range(view_count)])

    def owner_scratch(parts):
        return [chunked, chunked, ((chunks // 2 * ROWS, parts * WIDE), BF16), arrived]

    def tile_scratch(parts):
        return [arrived, ((devices // 2 * ROWS, parts * WIDE), BF16), terms]

    def pull(mode, image, maps_here, extra, outs):
        here, ordered = maps_here
        return call(
            functools.partial(tile_pull, tile_meta, mode),
            [payload] + outs,
            [
                images,
                ((blocks // TOGETHER, PIXELS, 4 * TOGETHER * ROWS), BF16),
                listed,
                listed,
                ((2, devices // 2 * ROWS, LANES), F32),
            ],
            "pull",
            image, here, shifted(here, -1), shifted(ordered, 1), pair_row, ta, onehot, moments, late, ax, ay,
            theta, weight, pieces, rho, left, *extra,
        )

    indices = ((devices, LANES), jnp.int32)
    sent, sa, sends = call(
        functools.partial(first_owner, owner_meta),
        [payload, indices, ((WIDE, devices * LANES), BF16)],
        owner_scratch(3) + [indices, indices],
        "project",
        attributes, send_index[0],
    )
    listing = ((blocks, LANES), jnp.int32)
    ta, ax, ay, onehot, basis, moments, early, late = call(
        functools.partial(tables, tile_meta),
        [
            listing,
            ((blocks, LANES), F32),
            ((blocks, LANES), F32),
            ((WIDE, blocks * LANES), BF16),
            ((PIXELS, 32), BF16),
            ((ROWS, 2 * PIXELS), BF16),
            ((3 * LANES, LANES), BF16),
            ((2 * LANES, LANES), BF16),
        ],
        [((tiles, LANES), jnp.int32), listing],
        "tables",
        tile_list, tile_anchor,
    )
    theta, weight, pieces, rho, left, image, here, ordered = call(
        functools.partial(tile_forward, tile_meta),
        [listed, field, ((blocks, PIXELS, WIDE), BF16), field, ((blocks * 32, WIDE), BF16), images, maps, maps],
        tile_scratch(3),
        "forward",
        exchange(sent), ta, onehot, basis, early, ax, ay, target, pair_row,
    )
    (sent,) = pull(0, image, (here, ordered), (), [])
    sent, residual, direction = call(
        functools.partial(owner_step, owner_meta, True),
        [payload, owned, owned],
        owner_scratch(2) + [summed, chunked, chunked],
        "gradient",
        exchange(sent), attributes, preconditioner, sa, sends,
    )
    image, here, ordered, first_sums = call(
        functools.partial(tile_tangent, tile_meta, True),
        [images, maps, maps, scalars],
        tile_scratch(2) + [listed],
        "tangent",
        exchange(sent), ta, onehot, basis, early, ax, ay, pair_row, theta, weight, pieces, rho, left,
    )
    (sent,) = pull(1, image, (here, ordered), (direction,), [])
    sent, residual, update, scaled = call(
        functools.partial(owner_step, owner_meta, False),
        [payload, owned, owned, owned],
        owner_scratch(2) + [summed, chunked, chunked],
        "step",
        exchange(sent), attributes, preconditioner, sa, sends, residual, direction, first_sums,
    )
    image, here, ordered, sums = call(
        functools.partial(tile_tangent, tile_meta, False),
        [images, maps, maps, scalars],
        tile_scratch(2) + [listed],
        "tangent_next",
        exchange(sent), ta, onehot, basis, early, ax, ay, pair_row, theta, weight, pieces, rho, left, image, first_sums,
    )
    sent, direction = pull(2, image, (here, ordered), (scaled, direction, sums), [owned])
    update, residual = call(
        functools.partial(last_owner, owner_meta),
        [owned, owned],
        [chunked, arrived, summed, chunked],
        "finish",
        exchange(sent), attributes, sa, sends, residual, update, direction, sums,
    )
    return (update, residual)


def solution(mesh):
    in_specs = (
        P(None, ("cell", "view")),
        P(None, ("cell", "view")),
        P(("cell", "view"), None, None),
        P(None, None, ("cell", "view")),
        P(("cell", "view"), None, None),
        P(("cell", "view"), None),
        P(("cell", "view")),
    )
    out_specs = (P(None, ("cell", "view")), P(None, ("cell", "view")))
    return jax.shard_map(local, mesh=mesh, in_specs=in_specs, out_specs=out_specs, check_vma=False)
```

```python
import functools
import math

import jax
import jax.numpy as jnp
from jax import lax
from jax.experimental import pallas as pl
from jax.experimental.pallas import tpu as pltpu
from jax.sharding import PartitionSpec as P

ITERS = 2
DAMPING = 0.5
PRIOR_WEIGHT = 0.3
DILATION = 0.3

F32 = jnp.float32
BF16 = jnp.bfloat16
LANES = 128
ROWS = 16
SCALAR = 6
ACTIVE = (0, 1, 2, 3, 4, 5, 6, 8, 9, 10, 11, 12)
KSLOTS = 64
PIXELS = 256
WIDE = 2 * LANES
TOGETHER = 4
GROUP = 8
ATTRS = 14


def camera_axes():
    tilt_cos, tilt_sin = (math.cos(0.3), math.sin(0.3))
    turn_cos, turn_sin = (math.cos(0.2), math.sin(0.2))
    return (
        (turn_cos, turn_sin * tilt_sin, turn_sin * tilt_cos),
        (0.0, tilt_cos, -tilt_sin),
        (-turn_sin, turn_cos * tilt_sin, turn_cos * tilt_cos),
    )


CAM = camera_axes()


def payload_rows(slots):
    return -(-len(ACTIVE) * slots // LANES)


def iota(shape, dim):
    return lax.broadcasted_iota(jnp.int32, shape, dim)


def split(value, parts):
    pieces = []
    for _ in range(parts - 1):
        piece = value.astype(BF16)
        pieces.append(piece)
        value = value - piece.astype(F32)
    pieces.append(value.astype(BF16))
    return pieces


def dot(a, b):
    return jnp.dot(a, b, preferred_element_type=F32)


def dot_nt(a, b):
    return lax.dot_general(a, b, (((1,), (1,)), ((), ())), preferred_element_type=F32)


def total(value):
    return jnp.sum(jnp.sum(value, axis=0, keepdims=True), axis=1, keepdims=True)


def pack(feature, out_ref, count, slots):
    depth = payload_rows(slots)
    lane = iota((count, LANES), 1)
    rows = [jnp.zeros((count, LANES), F32) for _ in range(depth)]
    for place, row in enumerate(ACTIVE):
        value = feature(row)
        at, offset = divmod(place * slots, LANES)
        end = offset + slots
        if offset:
            value = pltpu.roll(value, offset, 1)
        rows[at] = jnp.where((lane >= offset) & (lane < end), value, rows[at])
        if end > LANES:
            rows[at + 1] = jnp.where(lane < end - LANES, value, rows[at + 1])
    for at in range(depth):
        out_ref[pl.ds(at, count, stride=depth), :] = rows[at]


def unpack(in_ref, count, slots):
    depth = payload_rows(slots)
    lane = iota((count, LANES), 1)
    rows = [in_ref[pl.ds(at, count, stride=depth), :] for at in range(depth)]
    features = {}
    for place, row in enumerate(ACTIVE):
        at, offset = divmod(place * slots, LANES)
        value = rows[at]
        if offset + slots > LANES:
            value = jnp.where(lane >= offset, value, rows[at + 1])
        if offset:
            value = pltpu.roll(value, LANES - offset, 1)
        features[row] = jnp.where(lane < slots, value, 0.0)
    return features


def put_features(features, ref, count):
    ref[...] = jnp.zeros(ref.shape, F32)
    for row, value in features.items():
        ref[pl.ds(row, count, stride=ROWS), :] = value


def put_halves(chunk_index, lane, count, valid, a_ref, b_ref):
    half = count // 2
    upper = chunk_index >= half
    a_ref[...] = jnp.where(valid, jnp.where(upper, chunk_index - half, chunk_index), -1)
    b_ref[...] = jnp.where(valid, jnp.where(upper, LANES + lane, lane), -1)


def put_onehot(index_b, blocks, out_ref):
    wide = iota((WIDE, LANES), 0)
    for i in range(blocks):
        hit = jnp.where(wide == index_b[i : i + 1, :], 1.0, 0.0)
        out_ref[:, i * LANES : (i + 1) * LANES] = hit.astype(BF16)


def rows_of(index_ref, step):
    first = step * TOGETHER
    return jnp.concatenate([index_ref[pl.ds(first + i, 1), :] for i in range(TOGETHER)], axis=1)


def lanes_of(ref, step):
    width = TOGETHER * LANES
    return ref[:, pl.ds(pl.multiple_of(step * width, width), width)]


def whole(blocks):
    return min(blocks // TOGETHER, 8)


def gather(source_ref, chunks, index_a, onehot_ref, blocks, parts, lhs_ref, out_ref):
    half = chunks // 2
    for part, piece in enumerate(split(source_ref[...], parts)):
        for side in range(2):
            lhs_ref[:, part * WIDE + side * LANES : part * WIDE + (side + 1) * LANES] = piece[
                side * half * ROWS : (side + 1) * half * ROWS
            ]

    def body(step, carry):
        which = rows_of(index_a, step)
        onehot = lanes_of(onehot_ref, step)
        product = dot(lhs_ref[...], jnp.concatenate([onehot] * parts, axis=0))
        picked = product[:ROWS]
        for a in range(1, half):
            picked = jnp.where(which == a, product[a * ROWS : (a + 1) * ROWS], picked)
        for i in range(TOGETHER):
            start = pl.multiple_of((step * TOGETHER + i) * ROWS, ROWS)
            out_ref[pl.ds(start, ROWS), :] = picked[:, i * LANES : (i + 1) * LANES]
        return carry

    lax.fori_loop(0, blocks // TOGETHER, body, 0, unroll=whole(blocks))


def scatter(source_ref, chunks, index_a, onehot_ref, blocks, acc_ref, unroll):
    half = chunks // 2
    acc_ref[...] = jnp.zeros(acc_ref.shape, F32)

    def body(step, carry):
        left = [[], []]
        for i in range(TOGETHER):
            at = step * TOGETHER + i
            value = source_ref[pl.ds(pl.multiple_of(at * ROWS, ROWS), ROWS), :]
            which = jnp.broadcast_to(index_a[pl.ds(at, 1), :], (ROWS, LANES)).astype(F32).astype(BF16)
            masks = [which == jnp.asarray(a, BF16) for a in range(half)]
            for part, piece in enumerate(split(value, 2)):
                nothing = jnp.zeros_like(piece)
                left[part].append(jnp.concatenate([jnp.where(mask, piece, nothing) for mask in masks], axis=0))
        onehot = lanes_of(onehot_ref, step)
        product = dot_nt(jnp.concatenate(left[0] + left[1], axis=1), jnp.concatenate([onehot, onehot], axis=1))
        for side in range(2):
            acc_ref[side] += column(product, side)
        return carry

    lax.fori_loop(0, blocks // TOGETHER, body, 0, unroll=unroll)


def wide_reader(ref, count):
    half = count // 2
    return lambda row: jnp.concatenate(
        [ref[side, pl.ds(row, half, stride=ROWS), :] for side in range(2)], axis=0
    )


def geometry(attr):
    e3, e5, e8 = jnp.exp(attr(3)), jnp.exp(attr(5)), jnp.exp(attr(8))
    a4, a6, a7, a9 = attr(4), attr(6), attr(7), attr(9)
    m = [
        (
            CAM[r][0] * e3 + CAM[r][1] * a4 + CAM[r][2] * a6,
            CAM[r][1] * e5 + CAM[r][2] * a7,
            CAM[r][2] * e8,
        )
        for r in range(2)
    ]
    sxx = m[0][0] * m[0][0] + m[0][1] * m[0][1] + m[0][2] * m[0][2] + DILATION
    sxy = m[0][0] * m[1][0] + m[0][1] * m[1][1] + m[0][2] * m[1][2]
    syy = m[1][0] * m[1][0] + m[1][1] * m[1][1] + m[1][2] * m[1][2] + DILATION
    inverse = 1.0 / (sxx * syy - sxy * sxy)
    return {
        "e": (e3, e5, e8),
        "m": m,
        "q": (syy * inverse, -sxy * inverse, sxx * inverse),
        "fade": 1.0 / (1.0 + jnp.exp(a9)),
        "a9": a9,
    }


def place(value):
    return [CAM[r][0] * value(0) + CAM[r][1] * value(1) + CAM[r][2] * value(2) for r in range(3)]


def project(attr, geo):
    x, y, z = place(attr)
    a9 = geo["a9"]
    shade = math.log(0.99) - (jnp.maximum(-a9, 0.0) + jnp.log(1.0 + jnp.exp(-jnp.abs(a9))))
    rows = {0: x, 1: y, 12: z, 2: geo["q"][0], 3: geo["q"][1], 4: geo["q"][2], 5: shade}
    for band in range(4):
        rows[8 + band] = attr(10 + band)
    return rows


def project_tangent(v, geo):
    x, y, z = place(v)
    (e3, e5, e8), m, (qxx, qxy, qyy) = geo["e"], geo["m"], geo["q"]
    v3, v5, v8 = e3 * v(3), e5 * v(5), e8 * v(8)
    d = [
        (
            CAM[r][0] * v3 + CAM[r][1] * v(4) + CAM[r][2] * v(6),
            CAM[r][1] * v5 + CAM[r][2] * v(7),
            CAM[r][2] * v8,
        )
        for r in range(2)
    ]
    sxx = 2.0 * (m[0][0] * d[0][0] + m[0][1] * d[0][1] + m[0][2] * d[0][2])
    syy = 2.0 * (m[1][0] * d[1][0] + m[1][1] * d[1][1] + m[1][2] * d[1][2])
    sxy = sum(m[0][c] * d[1][c] + d[0][c] * m[1][c] for c in range(3))
    rows = {
        0: x,
        1: y,
        12: z,
        2: -(qxx * qxx * sxx + 2.0 * qxx * qxy * sxy + qxy * qxy * syy),
        3: -(qxx * qxy * sxx + (qxx * qyy + qxy * qxy) * sxy + qxy * qyy * syy),
        4: -(qxy * qxy * sxx + 2.0 * qxy * qyy * sxy + qyy * qyy * syy),
        5: geo["fade"] * v(9),
    }
    for band in range(4):
        rows[8 + band] = v(10 + band)
    return rows


def project_cotangent(t, geo):
    (e3, e5, e8), m, (qxx, qxy, qyy) = geo["e"], geo["m"], geo["q"]
    bxx, bxy, byy = t(2), t(3), t(4)
    sxx = -(qxx * qxx * bxx + qxx * qxy * bxy + qxy * qxy * byy)
    sxy = -(2.0 * qxx * qxy * bxx + (qxx * qyy + qxy * qxy) * bxy + 2.0 * qxy * qyy * byy)
    syy = -(qxy * qxy * bxx + qxy * qyy * bxy + qyy * qyy * byy)
    n0 = [2.0 * sxx * m[0][c] + sxy * m[1][c] for c in range(3)]
    n1 = [2.0 * syy * m[1][c] + sxy * m[0][c] for c in range(3)]
    x, y, z = t(0), t(1), t(12)
    out = {j: CAM[0][j] * x + CAM[1][j] * y + CAM[2][j] * z for j in range(3)}
    out[3] = e3 * (CAM[0][0] * n0[0] + CAM[1][0] * n1[0])
    out[4] = CAM[0][1] * n0[0] + CAM[1][1] * n1[0]
    out[5] = e5 * (CAM[0][1] * n0[1] + CAM[1][1] * n1[1])
    out[6] = CAM[0][2] * n0[0] + CAM[1][2] * n1[0]
    out[7] = CAM[0][2] * n0[1] + CAM[1][2] * n1[1]
    out[8] = e8 * (CAM[0][2] * n0[2] + CAM[1][2] * n1[2])
    out[9] = geo["fade"] * t(5)
    for band in range(4):
        out[10 + band] = t(8 + band)
    return out


def to_chunks(ref, chunk_ref, chunks):
    for a in range(chunks):
        chunk_ref[a * ROWS : a * ROWS + ATTRS, :] = ref[:, a * LANES : (a + 1) * LANES]


def reader(ref, count):
    return lambda row: ref[pl.ds(row, count, stride=ROWS), :]


def chunk(ref, a):
    return ref[a * ROWS : a * ROWS + ATTRS, :]


def send_rows(rows, scalar, meta, sa_ref, so_ref, source_ref, lhs_ref, sent_ref, out_ref, parts):
    chunks, devices, slots = meta
    put_features(rows, source_ref, chunks)
    gather(source_ref, chunks, sa_ref, so_ref, devices, parts, lhs_ref, sent_ref)

    def feature(row):
        if row == SCALAR:
            return jnp.broadcast_to(scalar, (devices, LANES))
        return sent_ref[pl.ds(row, devices, stride=ROWS), :]

    pack(feature, out_ref, devices, slots)


def first_owner(
    meta, attr_ref, send_ref, out_ref, sa_ref, sb_ref, chunk_ref, source_ref, lhs_ref, sent_ref, so_ref, ids_ref
):
    chunks, devices, slots = meta
    ids_ref[...] = jnp.full(ids_ref.shape, -1, jnp.int32)
    ids_ref[:, :slots] = send_ref[0]
    ids = ids_ref[...]
    put_halves(ids >> 7, ids & (LANES - 1), chunks, ids >= 0, sa_ref, sb_ref)
    put_onehot(sb_ref, devices, so_ref)
    to_chunks(attr_ref, chunk_ref, chunks)
    attr = reader(chunk_ref, chunks)
    rows = project(attr, geometry(attr))
    send_rows(rows, jnp.zeros((1, 1), F32), meta, sa_ref, so_ref, source_ref, lhs_ref, sent_ref, out_ref, 3)


def receive_cotangent(meta, recv_ref, sa_ref, so_ref, sent_ref, acc_ref, grad_ref, geo, unroll):
    chunks, devices, slots = meta
    features = unpack(recv_ref, devices, slots)
    put_features(features, sent_ref, devices)
    scatter(sent_ref, chunks, sa_ref, so_ref, devices, acc_ref, unroll)
    for j, value in project_cotangent(wide_reader(acc_ref, chunks), geo).items():
        grad_ref[pl.ds(j, chunks, stride=ROWS), :] = value
    return features[SCALAR]


def first_lane(value):
    return total(jnp.where(iota(value.shape, 1) == 0, value, 0.0))


def apply_scaling(pre_ref, source_ref, a):
    result = None
    for i in range(ATTRS):
        term = pre_ref[i, :, a * LANES : (a + 1) * LANES] * source_ref[a * ROWS + i : a * ROWS + i + 1, :]
        result = term if result is None else result + term
    return result


def owner_step(
    meta, first, recv_ref, attr_ref, pre_ref, sa_ref, so_ref, *rest
):
    if first:
        (out_ref, res_out, dir_out, chunk_ref, source_ref, lhs_ref, sent_ref, acc_ref, grad_ref, dir_ref) = rest
    else:
        (
            res_in, dir_in, sc_ref,
            out_ref, res_out, sol_out, dir_out,
            chunk_ref, source_ref, lhs_ref, sent_ref, acc_ref, grad_ref, dir_ref,
        ) = rest
    chunks, devices, slots = meta
    to_chunks(attr_ref, chunk_ref, chunks)
    attr = reader(chunk_ref, chunks)
    geo = geometry(attr)
    scalars = receive_cotangent(meta, recv_ref, sa_ref, so_ref, sent_ref, acc_ref, grad_ref, geo, 4)
    if not first:
        step = sc_ref[0:1, 0:1] / first_lane(scalars)
    norm = jnp.zeros((ATTRS, LANES), F32)
    for a in range(chunks):
        here = slice(a * LANES, (a + 1) * LANES)
        if first:
            residual = -chunk(grad_ref, a)
        else:
            before = dir_in[:, here]
            image = chunk(grad_ref, a) + DAMPING * before
            residual = res_in[:, here] - step * image
            sol_out[:, here] = step * before
        res_out[:, here] = residual
        grad_ref[a * ROWS : a * ROWS + ATTRS, :] = residual
        scaled = apply_scaling(pre_ref, grad_ref, a)
        dir_out[:, here] = scaled
        dir_ref[a * ROWS : a * ROWS + ATTRS, :] = scaled
        norm = norm + residual * scaled
    rows = project_tangent(reader(dir_ref, chunks), geo)
    send_rows(rows, total(norm), meta, sa_ref, so_ref, source_ref, lhs_ref, sent_ref, out_ref, 2)


def last_owner(
    meta, recv_ref, attr_ref, sa_ref, so_ref, res_in, sol_in, dir_in, sc_ref,
    sol_out, res_out, chunk_ref, sent_ref, acc_ref, grad_ref,
):
    chunks, devices, slots = meta
    to_chunks(attr_ref, chunk_ref, chunks)
    geo = geometry(reader(chunk_ref, chunks))
    scalars = receive_cotangent(meta, recv_ref, sa_ref, so_ref, sent_ref, acc_ref, grad_ref, geo, whole(devices))
    step = sc_ref[0:1, 0:1] / first_lane(scalars)
    for a in range(chunks):
        here = slice(a * LANES, (a + 1) * LANES)
        direction = dir_in[:, here]
        image = chunk(grad_ref, a) + DAMPING * direction
        sol_out[:, here] = sol_in[:, here] + step * direction
        res_out[:, here] = res_in[:, here] - step * image


def pixel_basis(shape, pixel_dim, term_dim):
    pixel, term = iota(shape, pixel_dim), iota(shape, term_dim) & 7
    x = (pixel & 15).astype(F32) - 7.5
    y = (pixel >> 4).astype(F32) - 7.5
    value = jnp.zeros(shape, F32)
    for m, field in enumerate((jnp.ones(shape, F32), x, y, x * x, x * y, y * y)):
        value = jnp.where(term == m, field, value)
    return value


def triangle(rows, later):
    shape = (rows, LANES)
    row, column = iota(shape, 0) & (LANES - 1), iota(shape, 1)
    same = (row >> 6) == (column >> 6)
    order = (row > column) if later else (row < column)
    return jnp.where(same & order, 1.0, 0.0).astype(BF16)


def put_terms(terms, ref, blocks):
    ref[...] = jnp.zeros(ref.shape, F32)
    for m, term in enumerate(terms):
        ref[pl.ds(m, blocks, stride=8), :] = term


def tables(
    meta, list_ref, anchor_ref, pair_ref, sb_ref,
    ta_ref, ax_ref, ay_ref, onehot_ref, so_ref, to_past_ref, of_next_ref, basis_ref, moment_ref, early_ref, late_ref,
    wide_ref, tb_ref,
):
    blocks, devices, slots = meta
    put_onehot(sb_ref, devices, so_ref)
    tiles = 2 * blocks
    partner = jnp.where(iota((tiles, tiles), 0) == pair_ref[...], 1.0, 0.0)
    to_past_ref[...] = partner.astype(BF16)
    of_next_ref[...] = partner.T.astype(BF16)
    wide_ref[:, :KSLOTS] = list_ref[...]
    even, odd = (wide_ref[pl.ds(side, blocks, stride=2), :] for side in range(2))
    lane = iota((blocks, LANES), 1)
    entries = jnp.where(lane < KSLOTS, even, pltpu.roll(odd, KSLOTS, 1))
    source = ((entries.astype(F32) + 0.5) * (1.0 / slots)).astype(jnp.int32)
    put_halves(source, entries - slots * source, devices, entries >= 0, ta_ref, tb_ref)
    put_onehot(tb_ref, blocks, onehot_ref)
    tile, block = iota((blocks, 2 * blocks), 1), iota((blocks, 2 * blocks), 0)
    for axis, ref in enumerate((ax_ref, ay_ref)):
        sides = [
            jnp.sum(jnp.where(tile == 2 * block + side, anchor_ref[axis : axis + 1, :], 0.0), axis=1, keepdims=True)
            for side in range(2)
        ]
        ref[...] = jnp.where(lane < KSLOTS, sides[0], sides[1])
    basis = pixel_basis((PIXELS, 32), 0, 1)
    basis_ref[...] = jnp.where(iota((PIXELS, 32), 1) < 24, basis, 0.0).astype(BF16)
    moments = pixel_basis((ROWS, PIXELS), 1, 0)
    moments = jnp.where(iota((ROWS, PIXELS), 0) < 8, moments, 0.0).astype(BF16)
    moment_ref[...] = jnp.concatenate([moments, moments], axis=1)
    early_ref[...] = triangle(3 * LANES, False)
    late_ref[...] = triangle(2 * LANES, True)


def two_tiles(value):
    low = iota((8, LANES), 1) < KSLOTS
    return jnp.concatenate([jnp.where(low, value, 0.0), jnp.where(low, 0.0, value)], axis=0)


def stacked_lhs(value):
    high, low = split(value, 2)
    return jnp.concatenate(
        [jnp.concatenate([high, high], axis=1), jnp.concatenate([low, jnp.zeros_like(low)], axis=1)], axis=0
    )


def fold(value):
    half = value.shape[0] // 2
    return value[:half] + value[half:]


def side_by_side(value, parts):
    return jnp.concatenate(split(value, parts), axis=1)


def local_place(theta, ax_ref, ay_ref):
    return theta(0) - ax_ref[...] - 8.0, theta(1) - ay_ref[...] - 8.0


def send_order(pr_ref, depth, ds_ref):
    ds_ref[...] = sum(dot(pr_ref[...], piece) for piece in split(depth, 3))


def receive_rows(meta, recv_ref, ta_ref, to_ref, source_ref, lhs_ref, out_ref, parts):
    blocks, devices, slots = meta
    features = unpack(recv_ref, devices, slots)
    put_features(features, source_ref, devices)
    gather(source_ref, devices, ta_ref, to_ref, blocks, parts, lhs_ref, out_ref)
    return features[SCALAR]


def coefficients(term_ref, first):
    columns = []
    for i in range(GROUP):
        value = term_ref[pl.ds(pl.multiple_of((first + i) * 8, 8), 8), :]
        pieces = [piece.astype(F32) for piece in split(value, 3)] + [jnp.zeros_like(value)]
        columns.append(jnp.concatenate(pieces, axis=0).astype(BF16))
    return jnp.concatenate(columns, axis=1)


def column(value, i):
    return value[:, i * LANES : (i + 1) * LANES]


def row_block(value, i):
    return value[i * PIXELS : (i + 1) * PIXELS]


def starts(first, count=TOGETHER):
    return [pl.multiple_of((first + i) * ROWS, ROWS) for i in range(count)]


def tile_forward(
    meta, recv_ref, ta_ref, to_ref, basis_ref, early_ref, ax_ref, ay_ref, target_ref, pr_ref,
    theta_ref, w_ref, ws_ref, rho_ref, left_ref, j_ref, d_ref, ds_ref,
    source_ref, lhs_ref, term_ref,
):
    blocks, devices, slots = meta
    receive_rows(meta, recv_ref, ta_ref, to_ref, source_ref, lhs_ref, theta_ref, 3)
    theta = reader(theta_ref, blocks)
    dx, dy = local_place(theta, ax_ref, ay_ref)
    qxx, qxy, qyy = theta(2), theta(3), theta(4)
    gx, gy = qxx * dx + qxy * dy, qxy * dx + qyy * dy
    terms = (theta(5) - 0.5 * (dx * gx + dy * gy), gx, gy, -0.5 * qxx, -qxy, -0.5 * qyy)
    put_terms(terms, term_ref, blocks)

    def body(step, carry):
        first = step * GROUP
        each = range(GROUP)
        product = dot(basis_ref[...], coefficients(term_ref, first))
        exponents = [column(product, i) for i in each]
        coverages = [jnp.exp(value) for value in exponents]
        logs = [jnp.log(1.0 - value) for value in coverages]
        for i in each:
            rho_ref[first + i] = jnp.exp(exponents[i] - logs[i])
        before = dot(jnp.concatenate([side_by_side(value, 3) for value in logs], axis=0), early_ref[...])
        lefts = []
        for i, start in enumerate(starts(first, GROUP)):
            left = stacked_lhs(two_tiles(theta_ref[pl.ds(start + 8, 8), :]))
            left_ref[pl.ds(pl.multiple_of((first + i) * 32, 32), 32), :] = left
            lefts.append(left)
        images = []
        for i in each:
            weight = jnp.exp(row_block(before, i)) * coverages[i]
            w_ref[first + i] = weight
            pieces = side_by_side(weight, 2)
            ws_ref[first + i] = pieces
            images.append(fold(dot_nt(lefts[i], pieces)))
        for i, start in enumerate(starts(first, GROUP)):
            image = images[i]
            j_ref[pl.ds(start, ROWS), :] = image
            j_ref[pl.ds(start, 4), :] = image[0:4] - target_ref[2 * (first + i)]
            j_ref[pl.ds(start + 8, 4), :] = image[8:12] - target_ref[2 * (first + i) + 1]
            d_ref[pl.ds(2 * (first + i), 1), :] = image[4:5]
            d_ref[pl.ds(2 * (first + i) + 1, 1), :] = image[12:13]
        return carry

    lax.fori_loop(0, blocks // GROUP, body, 0, unroll=min(blocks // GROUP, 4))
    send_order(pr_ref, d_ref[...], ds_ref)


def tile_tangent(
    meta, first_time, recv_ref, ta_ref, to_ref, basis_ref, early_ref, ax_ref, ay_ref, pr_ref,
    theta_ref, w_ref, ws_ref, rho_ref, left_ref, *rest
):
    if first_time:
        j_ref, d_ref, ds_ref, sc_ref, source_ref, lhs_ref, term_ref, dot_ref = rest
    else:
        j_in, sc_in, j_ref, d_ref, ds_ref, sc_ref, source_ref, lhs_ref, term_ref, dot_ref = rest
    blocks, devices, slots = meta
    norm = first_lane(receive_rows(meta, recv_ref, ta_ref, to_ref, source_ref, lhs_ref, dot_ref, 2))
    if not first_time:
        ratio = norm / sc_in[0:1, 0:1]
        sc_ref[8:16, :] = jnp.broadcast_to(ratio, (8, LANES))
    else:
        sc_ref[8:16, :] = jnp.zeros((8, LANES), F32)
    sc_ref[0:8, :] = jnp.broadcast_to(norm, (8, LANES))
    theta, tangent = reader(theta_ref, blocks), reader(dot_ref, blocks)
    dx, dy = local_place(theta, ax_ref, ay_ref)
    qxx, qxy, qyy = theta(2), theta(3), theta(4)
    gx, gy = qxx * dx + qxy * dy, qxy * dx + qyy * dy
    tx, ty, txx, txy, tyy = (tangent(row) for row in range(5))
    hx = txx * dx + txy * dy + qxx * tx + qxy * ty
    hy = txy * dx + tyy * dy + qxy * tx + qyy * ty
    constant = tangent(5) - 0.5 * (tx * gx + dx * hx + ty * gy + dy * hy)
    put_terms((constant, hx, hy, -0.5 * txx, -txy, -0.5 * tyy), term_ref, blocks)

    def body(step, carry):
        first = step * GROUP
        each = range(GROUP)
        product = dot(basis_ref[...], coefficients(term_ref, first))
        changes = [column(product, i) for i in each]
        scaled = [side_by_side(rho_ref[first + i] * changes[i], 2) for i in each]
        before = dot(jnp.concatenate(scaled, axis=0), early_ref[: 2 * LANES, :])
        images = []
        for i, start in enumerate(starts(first, GROUP)):
            change = w_ref[first + i] * (changes[i] - row_block(before, i))
            left = left_ref[pl.ds(pl.multiple_of((first + i) * 32, 32), 32), :]
            left_change = stacked_lhs(two_tiles(dot_ref[pl.ds(start + 8, 8), :]))
            images.append(
                fold(
                    dot_nt(
                        jnp.concatenate([left, left_change], axis=1),
                        jnp.concatenate([side_by_side(change, 2), ws_ref[first + i]], axis=1),
                    )
                )
            )
        for i, start in enumerate(starts(first, GROUP)):
            image = images[i]
            if not first_time:
                image = image + ratio * j_in[pl.ds(start, ROWS), :]
            j_ref[pl.ds(start, ROWS), :] = image
            d_ref[pl.ds(2 * (first + i), 1), :] = image[4:5]
            d_ref[pl.ds(2 * (first + i) + 1, 1), :] = image[12:13]
        return carry

    lax.fori_loop(0, blocks // GROUP, body, 0, unroll=min(blocks // GROUP, 4))
    send_order(pr_ref, d_ref[...], ds_ref)


def tile_pull(
    meta, mode, j_ref, d_ref, next_ref, past_ref, pr_ref, ta_ref, to_ref, moment_ref, late_ref, ax_ref, ay_ref,
    theta_ref, w_ref, ws_ref, rho_ref, left_ref, *rest
):
    if mode == 0:
        out_ref, cot_ref, turned_ref, term_ref, bar_ref, acc_ref = rest
    elif mode == 1:
        dir_in, out_ref, cot_ref, turned_ref, term_ref, bar_ref, acc_ref = rest
    else:
        scaled_in, dir_in, sc_ref, out_ref, dir_out, cot_ref, turned_ref, term_ref, bar_ref, acc_ref = rest
    blocks, devices, slots = meta
    tiles = 2 * blocks
    depth = d_ref[...]
    partner = sum(dot(pr_ref[...], piece) for piece in split(next_ref[...], 3))
    prior = PRIOR_WEIGHT * (depth - partner)
    depth_bar = PRIOR_WEIGHT * prior - PRIOR_WEIGHT * (PRIOR_WEIGHT * (past_ref[...] - depth))
    image = j_ref[...]
    cot_ref[...] = image
    for tile in range(tiles):
        cot_ref[tile * 8 + 4 : tile * 8 + 5, :] = depth_bar[tile : tile + 1, :]
    scalar = jnp.zeros((1, 1), F32)
    if mode:
        if mode == 1:
            direction = dir_in[...]
        else:
            direction = scaled_in[...] + sc_ref[8:9, 0:1] * dir_in[...]
            dir_out[...] = direction
        energy = jnp.where((iota(image.shape, 0) & 7) < 4, image * image, 0.0)
        scalar = total(energy) + total(prior * prior) + DAMPING * total(direction * direction)
    span = TOGETHER * ROWS
    for step in range(blocks // TOGETHER):
        high, low = split(cot_ref[step * span : (step + 1) * span, :], 2)
        turned = jnp.concatenate([high.astype(F32), low.astype(F32)], axis=0).T.astype(BF16)
        turned_ref[step] = jnp.concatenate([turned, turned], axis=1)
    low_lanes = iota((8, LANES), 1) < KSLOTS

    def body(step, carry):
        first = step * TOGETHER
        each = range(TOGETHER)
        nothing = jnp.zeros((ROWS, LANES), BF16)
        columns = []
        for i in each:
            left = left_ref[pl.ds(pl.multiple_of((first + i) * 32, 32), 32), :]
            pieces = (left[:ROWS, :LANES], left[:ROWS, :LANES], left[ROWS:, :LANES], nothing)
            columns.append(
                jnp.concatenate([piece if other == i else nothing for piece in pieces for other in each], axis=0)
            )
        pulled = dot(turned_ref[step], jnp.concatenate(columns, axis=1))
        shares = [w_ref[first + i] * column(pulled, i) for i in each]
        after = dot(jnp.concatenate([side_by_side(share, 2) for share in shares], axis=0), late_ref[...])
        bars = [shares[i] - rho_ref[first + i] * row_block(after, i) for i in each]
        moments = dot(
            moment_ref[...],
            jnp.concatenate([jnp.concatenate(split(bar, 2), axis=0) for bar in bars], axis=1),
        )
        for i, start in enumerate(starts(first)):
            cot_high, cot_low = split(cot_ref[pl.ds(start, ROWS), :], 2)
            left = jnp.concatenate(
                [
                    jnp.concatenate([cot_high, cot_high], axis=1),
                    jnp.concatenate([cot_low, jnp.zeros_like(cot_low)], axis=1),
                ],
                axis=0,
            )
            pieces = ws_ref[first + i]
            colour_bar = fold(dot(left, jnp.concatenate([pieces[:, :LANES], pieces[:, LANES:]], axis=0)))
            bar_ref[pl.ds(start + 8, 8), :] = jnp.where(low_lanes, colour_bar[0:8], colour_bar[8:16])
            term_ref[pl.ds(start, 8), :] = column(moments, i)[0:8]
        return carry

    lax.fori_loop(0, blocks // TOGETHER, body, 0, unroll=whole(blocks))
    theta, bars = reader(theta_ref, blocks), reader(term_ref, blocks)
    dx, dy = local_place(theta, ax_ref, ay_ref)
    qxx, qxy, qyy = theta(2), theta(3), theta(4)
    gx, gy = qxx * dx + qxy * dy, qxy * dx + qyy * dy
    b0 = bars(0)
    hx, hy = bars(1) - 0.5 * dx * b0, bars(2) - 0.5 * dy * b0
    values = (
        -0.5 * gx * b0 + qxx * hx + qxy * hy,
        -0.5 * gy * b0 + qxy * hx + qyy * hy,
        dx * hx - 0.5 * bars(3),
        dy * hx + dx * hy - bars(4),
        dy * hy - 0.5 * bars(5),
        b0,
        jnp.zeros_like(b0),
        jnp.zeros_like(b0),
    )
    for line, value in enumerate(values):
        bar_ref[pl.ds(line, blocks, stride=ROWS), :] = value
    scatter(bar_ref, devices, ta_ref, to_ref, blocks, acc_ref, whole(blocks))
    summed = wide_reader(acc_ref, devices)

    def feature(line):
        if line == SCALAR:
            return jnp.broadcast_to(scalar, (devices, LANES))
        return summed(line)

    pack(feature, out_ref, devices, slots)


def call(body, outs, scratch, name, *args):
    return pl.pallas_call(
        body,
        out_shape=[jax.ShapeDtypeStruct(shape, dtype) for shape, dtype in outs],
        scratch_shapes=[pltpu.VMEM(shape, dtype) for shape, dtype in scratch],
        compiler_params=pltpu.CompilerParams(vmem_limit_bytes=VMEM_LIMIT),
        name=name,
    )(*args)


VMEM_LIMIT = 40 * 1024 * 1024


def local(attributes, tile_anchor, target, preconditioner, send_index, tile_list, pair_index):
    view_count = lax.axis_size("view")
    devices = lax.axis_size("cell") * view_count
    slots = send_index.shape[2]
    gaussians = attributes.shape[1]
    tiles = tile_list.shape[0]
    chunks, blocks = gaussians // LANES, tiles * KSLOTS // LANES
    depth = payload_rows(slots)

    pair_row = pair_index.reshape(1, tiles)

    owner_meta = (chunks, devices, slots)
    tile_meta = (blocks, devices, slots)
    shape = (devices * depth, LANES)
    payload = (shape, F32)
    field = ((blocks, PIXELS, LANES), F32)
    owned = ((ATTRS, gaussians), F32)
    images, maps, scalars = ((blocks * ROWS, PIXELS), F32), ((tiles, PIXELS), F32), ((16, LANES), F32)
    chunked = ((chunks * ROWS, LANES), F32)
    summed = ((2, chunks // 2 * ROWS, LANES), F32)
    arrived = ((devices * ROWS, LANES), F32)
    listed = ((blocks * ROWS, LANES), F32)
    terms = ((blocks * 8, LANES), F32)

    def exchange(value):
        value = value.reshape(devices, 1, depth * LANES)
        value = lax.all_to_all(value, ("cell", "view"), split_axis=0, concat_axis=0, tiled=True)
        return value.reshape(shape)

    def shifted(value, by):
        return lax.ppermute(value, "view", [(i, (i + by) % view_count) for i in range(view_count)])

    def owner_scratch(parts):
        return [chunked, chunked, ((chunks // 2 * ROWS, parts * WIDE), BF16), arrived]

    def tile_scratch(parts):
        return [arrived, ((devices // 2 * ROWS, parts * WIDE), BF16), terms]

    def pull(mode, image, maps_here, extra, outs):
        here, ordered = maps_here
        return call(
            functools.partial(tile_pull, tile_meta, mode),
            [payload] + outs,
            [
                images,
                ((blocks // TOGETHER, PIXELS, 4 * TOGETHER * ROWS), BF16),
                listed,
                listed,
                ((2, devices // 2 * ROWS, LANES), F32),
            ],
            "pull",
            image, here, shifted(here, -1), shifted(ordered, 1), of_next, ta, onehot, moments, late, ax, ay,
            theta, weight, pieces, rho, left, *extra,
        )

    indices = ((devices, LANES), jnp.int32)
    indices = ((devices, LANES), jnp.int32)
    wide = ((WIDE, devices * LANES), BF16)
    sent, sa, sb = call(
        functools.partial(first_owner, owner_meta),
        [payload, indices, indices],
        owner_scratch(3) + [wide, indices],
        "project",
        attributes, send_index,
    )
    listing = ((blocks, LANES), jnp.int32)
    pairing = ((tiles, tiles), BF16)
    ta, ax, ay, onehot, sends, to_past, of_next, basis, moments, early, late = call(
        functools.partial(tables, tile_meta),
        [
            listing,
            ((blocks, LANES), F32),
            ((blocks, LANES), F32),
            ((WIDE, blocks * LANES), BF16),
            wide,
            pairing,
            pairing,
            ((PIXELS, 32), BF16),
            ((ROWS, 2 * PIXELS), BF16),
            ((3 * LANES, LANES), BF16),
            ((2 * LANES, LANES), BF16),
        ],
        [((tiles, LANES), jnp.int32), listing],
        "tables",
        tile_list, tile_anchor, pair_row, sb,
    )
    theta, weight, pieces, rho, left, image, here, ordered = call(
        functools.partial(tile_forward, tile_meta),
        [listed, field, ((blocks, PIXELS, WIDE), BF16), field, ((blocks * 32, WIDE), BF16), images, maps, maps],
        tile_scratch(3),
        "forward",
        exchange(sent), ta, onehot, basis, early, ax, ay, target, to_past,
    )
    (sent,) = pull(0, image, (here, ordered), (), [])
    sent, residual, direction = call(
        functools.partial(owner_step, owner_meta, True),
        [payload, owned, owned],
        owner_scratch(2) + [summed, chunked, chunked],
        "gradient",
        exchange(sent), attributes, preconditioner, sa, sends,
    )
    image, here, ordered, first_sums = call(
        functools.partial(tile_tangent, tile_meta, True),
        [images, maps, maps, scalars],
        tile_scratch(2) + [listed],
        "tangent",
        exchange(sent), ta, onehot, basis, early, ax, ay, to_past, theta, weight, pieces, rho, left,
    )
    (sent,) = pull(1, image, (here, ordered), (direction,), [])
    sent, residual, update, scaled = call(
        functools.partial(owner_step, owner_meta, False),
        [payload, owned, owned, owned],
        owner_scratch(2) + [summed, chunked, chunked],
        "step",
        exchange(sent), attributes, preconditioner, sa, sends, residual, direction, first_sums,
    )
    image, here, ordered, sums = call(
        functools.partial(tile_tangent, tile_meta, False),
        [images, maps, maps, scalars],
        tile_scratch(2) + [listed],
        "tangent_next",
        exchange(sent), ta, onehot, basis, early, ax, ay, to_past, theta, weight, pieces, rho, left, image, first_sums,
    )
    sent, direction = pull(2, image, (here, ordered), (scaled, direction, sums), [owned])
    update, residual = call(
        functools.partial(last_owner, owner_meta),
        [owned, owned],
        [chunked, arrived, summed, chunked],
        "finish",
        exchange(sent), attributes, sa, sends, residual, update, direction, sums,
    )
    return (update, residual)


def solution(mesh):
    in_specs = (
        P(None, ("cell", "view")),
        P(None, ("cell", "view")),
        P(("cell", "view"), None, None),
        P(None, None, ("cell", "view")),
        P(("cell", "view"), None, None),
        P(("cell", "view"), None),
        P(("cell", "view")),
    )
    out_specs = (P(None, ("cell", "view")), P(None, ("cell", "view")))
    return jax.shard_map(local, mesh=mesh, in_specs=in_specs, out_specs=out_specs, check_vma=False)
```
